32 devices in a mesh: fsdp: 16 (over z, y, core), seq: 2 (over x).
Axes of the slice: x: 2, y: 2, z: 4, core: 2. Of those that a mesh axis runs over, the one named last changes fastest.
Arguments:
- tokens: bfloat16 [16, 1024, 768], P('fsdp', 'seq'), may hold values from -6 to 6
- first_norm_gain: bfloat16 [768], P('fsdp'), may hold values from 0.099609375 to 1.8984375
- first_norm_shift: bfloat16 [768], P('fsdp'), may hold values from -3 to 3
- second_norm_gain: bfloat16 [768], P('fsdp'), may hold values from 0.099609375 to 1.8984375
- second_norm_shift: bfloat16 [768], P('fsdp'), may hold values from -3 to 3
- projection_weight: bfloat16 [768, 2304], P('fsdp'), may hold values from -10 to 10
- projection_bias: bfloat16 [2304], P('fsdp'), may hold values from -3 to 3
- output_weight: bfloat16 [768, 768], P('fsdp'), may hold values from -1.75 to 1.75
- output_bias: bfloat16 [768], P('fsdp'), may hold values from -3 to 3
- expand_weight: bfloat16 [768, 3072], P('fsdp'), may hold values from -0.21875 to 0.21875
- expand_bias: bfloat16 [3072], P('fsdp'), may hold values from -3 to 3
- contract_weight: bfloat16 [3072, 768], P('fsdp'), may hold values from -0.109375 to 0.109375
- contract_bias: bfloat16 [768], P('fsdp'), may hold values from -3 to 3
- cotangent: bfloat16 [16, 1024, 768], P('fsdp', 'seq'), may hold values from -6 to 6
Outputs:
- layer_output: bfloat16 [16, 1024, 768], P('fsdp', 'seq')
- tokens_grad: float32 [16, 1024, 768], P('fsdp', 'seq')
- grad_first_norm_gain: float32 [768], P('fsdp')
- grad_first_norm_shift: float32 [768], P('fsdp')
- grad_second_norm_gain: float32 [768], P('fsdp')
- grad_second_norm_shift: float32 [768], P('fsdp')
- grad_projection_weight: float32 [768, 2304], P('fsdp')
- grad_projection_bias: float32 [2304], P('fsdp')
- grad_output_weight: float32 [768, 768], P('fsdp')
- grad_output_bias: float32 [768], P('fsdp')
- grad_expand_weight: float32 [768, 3072], P('fsdp')
- grad_expand_bias: float32 [3072], P('fsdp')
- grad_contract_weight: float32 [3072, 768], P('fsdp')
- grad_contract_bias: float32 [768], P('fsdp')
The draws below stay inside these ranges and needn't reach their ends.
All inputs are finite; a program needn't handle non-finite values.
Results may differ from the reference program's by a relative error of at most 0.006.
The reference program's roundings to bfloat16 on the way count: a program that leaves them out, or rounds other values in their place, can miss the bound.
Values may be sent and summed in bfloat16 or wider, within the bound.
No kernel may reach another device: no remote copies, remote signals or barrier semaphores. Data moves between devices by JAX's collectives and lax.ppermute only.
A program may use at most 192 MiB of HBM per device.

```python
import jax
import jax.numpy as jnp
from jax import lax

D = 768
H = 12
HD = 64
FF = 3072
ROT = 16
LENGTH = 1024
SEQS = 16


def draw_projection_weight(key, part):
    first_key, second_key, third_key = jax.random.split(key, 3)
    factor = D ** (-0.5)
    query_part = jax.random.normal(first_key, (D, D), jnp.float32) * factor
    key_part = jax.random.normal(second_key, (D, D), jnp.float32) * factor
    value_part = jax.random.normal(third_key, (D, D), jnp.float32) * factor
    return jnp.concatenate([query_part, key_part, value_part], axis=1).astype(jnp.bfloat16)


def raised(drawn, own_key, source, target, shards_of, factor):
    def block_of(dim):
        return (jnp.arange(drawn.shape[dim]) // (drawn.shape[dim] // shards_of)).reshape((-1,) + (1,) * (drawn.ndim - 1 - dim))

    near = jax.random.permutation(own_key, shards_of)[block_of(target)]
    other_side = (block_of(target) + shards_of // 2) % shards_of
    return jnp.where((block_of(source) == near) | (block_of(source) == other_side), factor * drawn, drawn)


def block_scale(key, dims, cuts, smallest, largest):
    def one(dim, parts):
        draws = jax.random.uniform(jax.random.fold_in(jax.random.fold_in(key, 6), dim), (parts,), jnp.float32, smallest / len(cuts), largest / len(cuts))
        return jnp.repeat(jnp.exp(draws), dims[dim] // parts).reshape((-1,) + (1,) * (len(dims) - dim - 1))

    factor_of = one(*cuts[0])
    for cut in cuts[1:]:
        factor_of = factor_of * one(*cut)
    return factor_of


def noise(own_key, dims, spread, reach, shards=(), kind=jnp.bfloat16):
    factor_of = block_scale(own_key, dims, shards, -0.22, 0.18) if shards else 1.0
    array = jax.random.normal(own_key, dims, jnp.float32) * spread * factor_of
    return jnp.minimum(jnp.maximum(array, -reach), reach).astype(kind)


def gaussian_with(own_key, extent, deviation, most, cuts, heavy, kind=jnp.bfloat16):
    values = deviation * jax.random.normal(own_key, extent, jnp.float32)
    if cuts:
        values = values * block_scale(own_key, extent, cuts, -0.22, 0.18)
    return jnp.clip(raised(values, jax.random.fold_in(own_key, 3), *heavy), -most, most).astype(kind)


def setup_inputs(seed: int = 0) -> dict:
    keys = jax.random.split(jax.random.key(seed), 15)
    tokens = noise(keys[0], (SEQS, LENGTH, D), 1.0, 6.0, ((0, 16), (1, 2)))
    first_norm_gain = jnp.clip(1.0 + 0.18 * jax.random.normal(keys[1], (D,), jnp.float32), 0.099609375, 1.8984375).astype(jnp.bfloat16)
    first_norm_shift = noise(keys[2], (D,), 0.5, 3.0, ((0, 16),))
    second_norm_gain = jnp.clip(1.0 + 0.18 * jax.random.normal(keys[3], (D,), jnp.float32), 0.099609375, 1.8984375).astype(jnp.bfloat16)
    second_norm_shift = noise(keys[4], (D,), 0.5, 3.0, ((0, 16),))
    projection_weight = draw_projection_weight(jax.random.fold_in(keys[14], 71), 0)
    projection_bias = noise(keys[6], (3 * D,), 0.5, 3.0, ((0, 16),))
    output_weight = noise(keys[7], (D, D), (max(1, D * 16 // LENGTH)) ** -0.5, 1.75, ((0, 16),))
    output_bias = noise(keys[8], (D,), 0.5, 3.0, ((0, 16),))
    expand_weight = noise(keys[9], (D, FF), D ** -0.5, 0.21875, ((0, 16),))
    expand_bias = noise(keys[10], (FF,), 0.5, 3.0, ((0, 16),))
    contract_weight = noise(keys[11], (FF, D), FF ** -0.5, 0.109375, ((0, 16),))
    contract_bias = noise(keys[12], (D,), 0.5, 3.0, ((0, 16),))
    cotangent = gaussian_with(keys[13], (SEQS, LENGTH, D), 1.0, 6.0, ((0, 16), (1, 2)), (0, 2, 16, 2.0))
    return {"tokens": tokens, "first_norm_gain": first_norm_gain, "first_norm_shift": first_norm_shift, "second_norm_gain": second_norm_gain, "second_norm_shift": second_norm_shift, "projection_weight": projection_weight, "projection_bias": projection_bias, "output_weight": output_weight, "output_bias": output_bias, "expand_weight": expand_weight, "expand_bias": expand_bias, "contract_weight": contract_weight, "contract_bias": contract_bias, "cotangent": cotangent}


@jax.custom_vjp
def low(v):
    return lax.optimization_barrier(v.astype(jnp.bfloat16)).astype(jnp.float32)

@jax.custom_vjp
def low_back(v):
    return v

def low_keep(v):
    return (low(v), None)

def low_pass(kept, grad):
    return (grad,)

def back_keep(v):
    return (v, None)

def back_low(kept, grad):
    return (low(grad),)
low.defvjp(low_keep, low_pass)
low_back.defvjp(back_keep, back_low)
EPSILON = 1e-05
HIGHEST = lax.Precision.HIGHEST

def norm_apply(values, gain, shift):
    average = lax.optimization_barrier(jnp.mean(values, axis=-1, keepdims=True))
    centred = values - average
    variance = lax.optimization_barrier(jnp.mean(centred * centred, axis=-1, keepdims=True))
    return centred * lax.rsqrt(variance + EPSILON) * gain + shift

def rotary_tables(positions, rot_dims):
    half_dims = rot_dims // 2
    frequency = 10000.0 ** (-(2.0 * jnp.arange(half_dims, dtype=jnp.float32)) / rot_dims)
    angles = positions.astype(jnp.float32)[:, None] * frequency[None, :]
    return (jnp.cos(angles), jnp.sin(angles))

def rotate_heads(values, cosine_table, sine_table, heads, rot_dims):
    shaped = values.reshape(values.shape[:-1] + (heads, -1))
    half_dims = rot_dims // 2
    cosine_wide = cosine_table[:, None, :]
    sine_wide = sine_table[:, None, :]
    first_half = shaped[..., :half_dims]
    second_half = shaped[..., half_dims:rot_dims]
    remainder = shaped[..., rot_dims:]
    turned = jnp.concatenate([first_half * cosine_wide - second_half * sine_wide, second_half * cosine_wide + first_half * sine_wide, remainder], axis=-1)
    return turned.reshape(values.shape)

def attend_block(query_block, start, keys_all, values_all):
    raw = jnp.einsum('qhd,khd->hqk', query_block, keys_all, precision=HIGHEST)
    scores = low_back(raw) * 0.125
    query_pos = start + jnp.arange(query_block.shape[0], dtype=jnp.int32)
    key_pos = jnp.arange(keys_all.shape[0], dtype=jnp.int32)
    allowed = key_pos[None, :] <= query_pos[:, None]
    scores = jnp.where(allowed[None], scores, -1e+30)
    highest = lax.optimization_barrier(jnp.max(scores, axis=-1, keepdims=True))
    expo_vals = jnp.exp(scores - highest)
    probs = expo_vals / lax.optimization_barrier(jnp.sum(expo_vals, axis=-1, keepdims=True))
    weights = low(probs)
    return jnp.einsum('hqk,khd->qhd', weights, values_all, precision=HIGHEST)

def one_sequence(params, inputs):
    gain_one, shift_one, gain_two, shift_two, joint_matrix, joint_shift, output_matrix, output_shift, expand_matrix, expand_shift, contract_matrix, contract_shift = params
    full_length = inputs.shape[0]
    hidden_one = low(norm_apply(inputs, gain_one, shift_one))
    hidden_two = low(norm_apply(inputs, gain_two, shift_two))
    projected = low_back(jnp.dot(hidden_one, joint_matrix, precision=HIGHEST) + joint_shift)
    positions = jnp.arange(full_length, dtype=jnp.int32)
    cosine_table, sine_table = rotary_tables(positions, ROT)
    queries = low(low_back(rotate_heads(projected[:, :D], cosine_table, sine_table, H, ROT)))
    keys_all = low(low_back(rotate_heads(projected[:, D:2 * D], cosine_table, sine_table, H, ROT)))
    values_all = low(low_back(projected[:, 2 * D:]))
    queries = queries.reshape(full_length, H, HD)
    keys_all = keys_all.reshape(full_length, H, HD)
    values_all = values_all.reshape(full_length, H, HD)
    block_rows = min(512, full_length)
    block_count = full_length // block_rows
    starts = jnp.arange(block_count, dtype=jnp.int32) * block_rows
    query_blocks = queries.reshape(block_count, block_rows, H, HD)
    attend = jax.checkpoint(attend_block)
    context = lax.map(lambda pair: attend(pair[0], pair[1], keys_all, values_all), (query_blocks, starts))
    context = low(low_back(context.reshape(full_length, D)))
    attended = jnp.dot(context, output_matrix, precision=HIGHEST) + output_shift
    expanded = low_back(jnp.dot(hidden_two, expand_matrix, precision=HIGHEST) + expand_shift)
    activated = low(jax.nn.gelu(expanded, approximate=False))
    mixed = jnp.dot(activated, contract_matrix, precision=HIGHEST) + contract_shift
    return inputs + attended + mixed

def reference(tokens, first_norm_gain, first_norm_shift, second_norm_gain, second_norm_shift, projection_weight, projection_bias, output_weight, output_bias, expand_weight, expand_bias, contract_weight, contract_bias, cotangent):
    params = tuple((value.astype(jnp.float32) for value in (first_norm_gain, first_norm_shift, second_norm_gain, second_norm_shift, projection_weight, projection_bias, output_weight, output_bias, expand_weight, expand_bias, contract_weight, contract_bias)))
    stacked = tokens.astype(jnp.float32)
    stepper = jax.checkpoint(one_sequence)

    def forward(weights_all, sequences):
        return lax.map(lambda inputs: stepper(weights_all, inputs), sequences)
    result, pullback = jax.vjp(forward, params, stacked)
    grads, tokens_grad = pullback(cotangent.astype(jnp.float32))
    return (result.astype(jnp.bfloat16), tokens_grad, grads[0], grads[1], grads[2], grads[3], grads[4], grads[5], grads[6], grads[7], grads[8], grads[9], grads[10], grads[11])
```

```python
from functools import partial

import jax
import jax.numpy as jnp
import numpy as np
from jax import lax
from jax.experimental import pallas as pl
from jax.experimental.pallas import tpu as pltpu
from jax.sharding import PartitionSpec as P

D = 768
H = 12
HD = 64
FF = 3072
ROT = 16
EPSILON = 1e-05
LANES = 128
VECS = 6

F32 = jnp.float32
BF16 = jnp.bfloat16


def f32(value):
    return value.astype(F32)


def bf16(value):
    return value.astype(BF16)


RING_CHIPS = (0, 2, 4, 6, 7, 5, 3, 1)
RING_SIZE = 16


def ring_pairs(step):
    count = len(RING_CHIPS)
    return [
        (RING_CHIPS[i] * 2 + core, RING_CHIPS[(i + step) % count] * 2 + core)
        for i in range(count)
        for core in range(2)
    ]


CLOCKWISE = ring_pairs(1)
COUNTER = ring_pairs(-1)
CORE_SWAP = [(f, f ^ 1) for f in range(RING_SIZE)]
SIDE_SWAP = [(0, 1), (1, 0)]


def ring_table():
    table = np.zeros((RING_SIZE, 16), np.int32)
    for f in range(RING_SIZE):
        place = RING_CHIPS.index(f // 2)
        for distance in range(8):
            chip = RING_CHIPS[(place + distance) % 8]
            table[f, distance] = chip * 2 + f % 2
            table[f, 8 + distance] = chip * 2 + 1 - f % 2
    return table


def clockwise(value):
    return lax.ppermute(value, "fsdp", CLOCKWISE)


def counter(value):
    return lax.ppermute(value, "fsdp", COUNTER)


def core_swap(value):
    return lax.ppermute(value, "fsdp", CORE_SWAP)


def side_swap(value):
    return lax.ppermute(value, "seq", SIDE_SWAP)


def ring_gather(shard, split_axis):
    half = shard.shape[split_axis] // 2
    first = lax.slice_in_dim(shard, 0, half, axis=split_axis)
    del first
    right, left = shard, shard
    own = [shard]
    for _ in range(3):
        left, right = counter(left), clockwise(right)
        own += [left, right]
    own.append(clockwise(lax.slice_in_dim(right, 0, half, axis=split_axis)))
    own.append(counter(lax.slice_in_dim(left, half, 2 * half, axis=split_axis)))
    return own + [core_swap(piece) for piece in own]


PIECE_DISTANCES = (0, 1, 7, 2, 6, 3, 5, 4, 4)


def assemble(pieces, order, copies_of, out_shapes):
    count = len(pieces)

    def kernel(order_ref, *refs):
        ins, outs, sem = refs[:count], refs[count:-1], refs[-1]
        started = []
        for number in range(count):
            core, place = divmod(number, 9)
            device = order_ref[core * 8 + PIECE_DISTANCES[place]]
            part = {7: "a", 8: "b"}.get(place, "all")
            for source, out, target in copies_of(part, device):
                copy = pltpu.make_async_copy(
                    ins[number].at[source], outs[out].at[target], sem.at[len(started)]
                )
                copy.start()
                started.append(copy)
        for copy in started:
            copy.wait()

    sems = sum(
        len(copies_of({7: "a", 8: "b"}.get(number % 9, "all"), 0)) for number in range(count)
    )
    return pl.pallas_call(
        kernel,
        grid_spec=pltpu.PrefetchScalarGridSpec(
            num_scalar_prefetch=1,
            grid=(),
            in_specs=[pl.BlockSpec(memory_space=pl.ANY)] * count,
            out_specs=[pl.BlockSpec(memory_space=pltpu.VMEM)] * len(out_shapes),
            scratch_shapes=[pltpu.SemaphoreType.DMA((sems,))],
        ),
        out_shape=out_shapes,
        name="assemble",
    )(order, *pieces)


def ring_scatter(grads, core, order, axis):
    by_core = grads.reshape((8, 2) + grads.shape[1:])
    mine = lax.dynamic_index_in_dim(by_core, core, 1, keepdims=False)
    other = lax.dynamic_index_in_dim(by_core, 1 - core, 1, keepdims=False)
    wire = BF16
    summed = mine + f32(core_swap(other.astype(wire)))

    def own(distance):
        return lax.dynamic_index_in_dim(summed, order[distance] // 2, 0, keepdims=False)

    axis_size = grads.shape[1 + axis]
    half = axis_size // 2
    head = partial(lax.slice_in_dim, start_index=0, limit_index=half, axis=axis)
    tail = partial(lax.slice_in_dim, start_index=half, limit_index=axis_size, axis=axis)
    far = own(4)
    right = clockwise(head(far).astype(wire))
    left = counter(tail(far).astype(wire))
    near, back = own(3), own(5)
    right = jnp.concatenate([head(near) + f32(right), tail(near)], axis).astype(wire)
    left = jnp.concatenate([head(back), tail(back) + f32(left)], axis).astype(wire)
    right, left = clockwise(right), counter(left)
    right, left = (own(2) + f32(right)).astype(wire), (own(6) + f32(left)).astype(wire)
    right, left = clockwise(right), counter(left)
    right, left = (own(1) + f32(right)).astype(wire), (own(7) + f32(left)).astype(wire)
    right, left = clockwise(right), counter(left)
    return own(0) + f32(right) + f32(left)


def attention_kernel(
    side_ref, q_ref, k_ref, v_ref, up_ref, tables_ref, context_ref, grads_ref, dk_acc, dv_acc
):
    rows = q_ref.shape[0]
    half = rows // 2
    block = min(256, half)
    start_one = pl.multiple_of(side_ref[0] * half, half)
    start_two = pl.multiple_of((1 - side_ref[0]) * half, half)

    def natural(ref):
        return jnp.concatenate([ref[pl.ds(start_one, half), :], ref[pl.ds(start_two, half), :]], 0)

    q = natural(q_ref) * jnp.asarray(0.125, BF16)
    k = natural(k_ref)
    v = natural(v_ref)
    up = natural(up_ref)
    lane = lax.broadcasted_iota(jnp.int32, (1, LANES), 1)
    contract_last = (((1,), (1,)), ((), ()))
    contract_first = (((0,), (0,)), ((), ()))
    dk_acc[...] = jnp.zeros_like(dk_acc)
    dv_acc[...] = jnp.zeros_like(dv_acc)
    below = lax.broadcasted_iota(jnp.int32, (block, block), 0) <= lax.broadcasted_iota(
        jnp.int32, (block, block), 1
    )

    def rotate_back(values, start):
        cosine = tables_ref[0, pl.ds(start, values.shape[0]), :]
        plus = tables_ref[1, pl.ds(start, values.shape[0]), :]
        minus = tables_ref[2, pl.ds(start, values.shape[0]), :]
        return (
            values * cosine
            - pltpu.roll(values, LANES - 8, 1) * plus
            - pltpu.roll(values, 8, 1) * minus
        )

    def local(row):
        return pl.multiple_of(
            (start_one if row < half else start_two) + (row if row < half else row - half), block
        )

    for number in range(rows // block):
        low, high = number * block, (number + 1) * block
        context_total = None
        dq_total = None
        for head in range(LANES // HD):
            mask = (lane // HD == head).astype(BF16)
            q_head = q[low:high] * mask
            up_head = up[low:high] * mask
            k_head = k[:high] * mask
            v_head = v[:high] * mask
            scores = lax.dot_general(k[:high], q_head, contract_last, preferred_element_type=F32)
            diagonal = jnp.where(below, scores[low:high], -1e30)
            scores = diagonal if low == 0 else jnp.concatenate([scores[:low], diagonal], 0)
            highest = jnp.max(scores, axis=0, keepdims=True)
            expo = jnp.exp(scores - highest)
            total = jnp.sum(expo, axis=0, keepdims=True)
            probs = expo * (1.0 / total)
            weights = probs.astype(BF16)
            weights_grad = lax.dot_general(
                v[:high], up_head, contract_last, preferred_element_type=F32
            )
            inner = jnp.sum(probs * weights_grad, axis=0, keepdims=True)
            scores_grad = (probs * (weights_grad - inner)).astype(BF16)
            context = lax.dot_general(
                v_head, weights, contract_first, preferred_element_type=F32
            )
            dq = lax.dot_general(k_head, scores_grad, contract_first, preferred_element_type=F32)
            context_total = context if context_total is None else context_total + context
            dq_total = dq if dq_total is None else dq_total + dq
            dv_acc[:high, :] += jnp.dot(weights, up_head, preferred_element_type=F32)
            dk_acc[:high, :] += jnp.dot(scores_grad, q_head, preferred_element_type=F32)
        place = local(low)
        context_ref[pl.ds(place, block), :] = context_total.T.astype(BF16)
        dq_low = (dq_total.T * 0.125).astype(BF16).astype(F32)
        grads_ref[0, pl.ds(place, block), :] = rotate_back(dq_low, place).astype(BF16)
    for number in range(rows // block):
        low = number * block
        place = local(low)
        dk_low = dk_acc[low : low + block, :].astype(BF16).astype(F32)
        grads_ref[1, pl.ds(place, block), :] = rotate_back(dk_low, place).astype(BF16)
        grads_ref[2, pl.ds(place, block), :] = dv_acc[low : low + block, :].astype(BF16)


def attention(side, packed, up, tables):
    rows, columns = up.shape
    pairs = columns // LANES
    return pl.pallas_call(
        attention_kernel,
        grid_spec=pltpu.PrefetchScalarGridSpec(
            num_scalar_prefetch=1,
            grid=(pairs,),
            in_specs=[
                pl.BlockSpec((rows, LANES), lambda i, s: (0, i)),
                pl.BlockSpec((rows, LANES), lambda i, s: (0, pairs + i)),
                pl.BlockSpec((rows, LANES), lambda i, s: (0, 2 * pairs + i)),
                pl.BlockSpec((rows, LANES), lambda i, s: (0, i)),
                pl.BlockSpec((3, rows, LANES), lambda i, s: (0, 0, 0)),
            ],
            out_specs=[
                pl.BlockSpec((rows, LANES), lambda i, s: (0, i)),
                pl.BlockSpec((3, rows, LANES), lambda i, s: (0, 0, i)),
            ],
            scratch_shapes=[pltpu.VMEM((rows, LANES), F32), pltpu.VMEM((rows, LANES), F32)],
        ),
        out_shape=[
            jax.ShapeDtypeStruct((rows, columns), BF16),
            jax.ShapeDtypeStruct((3, rows, columns), BF16),
        ],
        compiler_params=pltpu.CompilerParams(dimension_semantics=("arbitrary",)),
        name="attention",
    )(side, packed, packed, packed, up, tables)


def project_kernel(tokens_ref, vec_ref, weight_ref, bias_ref, tables_ref, *outs):
    packed_ref, one_ref, two_ref = outs
    values = tokens_ref[...].astype(F32)
    average = jnp.mean(values, axis=-1, keepdims=True)
    centred = values - average
    variance = jnp.mean(centred * centred, axis=-1, keepdims=True)
    unit = centred * lax.rsqrt(variance + EPSILON)
    one = (unit * vec_ref[0:1, :] + vec_ref[1:2, :]).astype(BF16)
    one_ref[...] = one
    two_ref[...] = (unit * vec_ref[2:3, :] + vec_ref[3:4, :]).astype(BF16)
    projected = jnp.dot(one, weight_ref[...], preferred_element_type=F32) + bias_ref[...]
    columns = projected.shape[1]
    cosine, plus, minus = tables_ref[0], tables_ref[1], tables_ref[2]
    for low in range(0, columns, LANES):
        piece = projected[:, low : low + LANES]
        if low < columns * 2 // 3:
            piece = (
                piece * cosine
                + pltpu.roll(piece, LANES - 8, 1) * plus
                + pltpu.roll(piece, 8, 1) * minus
            )
        packed_ref[:, low : low + LANES] = piece.astype(BF16)


def project(tokens, vecs, weight, bias, tables):
    rows = tokens.shape[0]
    columns = weight.shape[1]
    block = min(256, rows)
    return pl.pallas_call(
        project_kernel,
        grid=(rows // block,),
        in_specs=[
            pl.BlockSpec((block, D), lambda i: (i, 0)),
            pl.BlockSpec((8, D), lambda i: (0, 0)),
            pl.BlockSpec((D, columns), lambda i: (0, 0)),
            pl.BlockSpec((1, columns), lambda i: (0, 0)),
            pl.BlockSpec((3, block, LANES), lambda i: (0, i, 0)),
        ],
        out_specs=[
            pl.BlockSpec((block, columns), lambda i: (i, 0)),
            pl.BlockSpec((block, D), lambda i: (i, 0)),
            pl.BlockSpec((block, D), lambda i: (i, 0)),
        ],
        out_shape=[
            jax.ShapeDtypeStruct((rows, columns), BF16),
            jax.ShapeDtypeStruct((rows, D), BF16),
            jax.ShapeDtypeStruct((rows, D), BF16),
        ],
        name="project",
    )(tokens, vecs, weight, bias, tables)


def rotary_lanes(positions):
    lane = jnp.arange(LANES, dtype=jnp.int32) % HD
    half = ROT // 2
    frequency = 10000.0 ** (-(2.0 * f32(lane % half)) / ROT)
    angles = f32(positions)[:, None] * frequency[None, :]
    cosine, sine = jnp.cos(angles), jnp.sin(angles)
    low = (lane < half)[None, :]
    high = ((lane >= half) & (lane < ROT))[None, :]
    return jnp.stack(
        [
            jnp.where(low | high, cosine, 1.0),
            jnp.where(low, -sine, 0.0),
            jnp.where(high, sine, 0.0),
        ]
    )


def body(
    tokens,
    first_norm_gain,
    first_norm_shift,
    second_norm_gain,
    second_norm_shift,
    projection_weight,
    projection_bias,
    output_weight,
    output_bias,
    expand_weight,
    expand_bias,
    contract_weight,
    contract_bias,
    cotangent,
):
    shards = lax.axis_size("fsdp")
    ring = shards == RING_SIZE
    me = lax.axis_index("fsdp")
    side = lax.axis_index("seq")
    rows_local = tokens.shape[1]
    depth = D // shards
    wide = FF // shards // 2
    half_d, half_ff = D // 2, FF // 2

    own_tokens, own_up = tokens[0], cotangent[0]
    token_rows = jnp.concatenate([own_tokens, side_swap(own_tokens)], 0)
    upstream = jnp.concatenate([own_up, side_swap(own_up)], 0)

    projection_half = lax.dynamic_index_in_dim(
        projection_weight.reshape(depth, 3, 2, half_d), side, 2, keepdims=False
    ).reshape(depth, 3 * half_d)
    expand_half = lax.dynamic_index_in_dim(
        expand_weight.reshape(depth, shards, 2, wide), side, 2, keepdims=False
    ).reshape(depth, half_ff)
    contract_half = lax.dynamic_slice_in_dim(contract_weight, side * wide, wide, 0)
    vectors = jnp.concatenate(
        [
            jnp.stack(
                [
                    first_norm_gain,
                    first_norm_shift,
                    second_norm_gain,
                    second_norm_shift,
                    output_bias,
                    contract_bias,
                ]
            ),
            projection_bias.reshape(3, depth),
            expand_bias.reshape(4, depth),
        ],
        0,
    )
    vectors = jnp.pad(vectors.T, ((0, 0), (0, LANES - vectors.shape[0])))
    first_shard = jnp.concatenate([projection_half, output_weight, vectors], 1)
    split = 3 * half_d
    if ring:
        order = lax.dynamic_index_in_dim(jnp.asarray(ring_table()), me, 0, keepdims=False)
        second_shard = jnp.concatenate(
            [expand_half[:, :D], expand_half[:, D:], contract_half], 0
        )
        first_pieces = ring_gather(first_shard, 1)
        second_pieces = ring_gather(second_shard, 0)
        middle = first_shard.shape[1] // 2

        def first_copies(part, device):
            rows = pl.ds(pl.multiple_of(device * depth, depth), depth)
            everything = pl.ds(0, depth)
            if part == "a":
                return [((everything, pl.ds(0, middle)), 0, (rows, pl.ds(0, middle)))]
            rest = [
                ((split, D), 1),
                ((split + D, LANES), 2),
            ]
            shift = middle if part == "b" else 0
            copies = [
                ((everything, pl.ds(shift * 0, split - shift)), 0, (rows, pl.ds(shift, split - shift)))
            ]
            for (start, size), out in rest:
                copies.append(
                    ((everything, pl.ds(start - shift, size)), out, (rows, pl.ds(0, size)))
                )
            return copies

        def second_copies(part, device):
            rows = pl.ds(pl.multiple_of(device * depth, depth), depth)
            low = ((pl.ds(0, depth), pl.ds(0, D)), 0, (rows, pl.ds(0, D)))
            high = ((pl.ds(depth, depth), pl.ds(0, D)), 0, (rows, pl.ds(D, D)))
            start = 0 if part == "b" else 2 * depth
            lines = pl.ds(pl.multiple_of(device * wide, wide), wide)
            last = ((pl.ds(start, wide), pl.ds(0, D)), 1, (lines, pl.ds(0, D)))
            return {"all": [low, high, last], "a": [low, high], "b": [last]}[part]

        projection_full, output_full, vector_full = assemble(
            first_pieces,
            order,
            first_copies,
            [
                jax.ShapeDtypeStruct((D, split), BF16),
                jax.ShapeDtypeStruct((D, D), BF16),
                jax.ShapeDtypeStruct((D, LANES), BF16),
            ],
        )
        expand_full, contract_full = assemble(
            second_pieces,
            order,
            second_copies,
            [
                jax.ShapeDtypeStruct((D, half_ff), BF16),
                jax.ShapeDtypeStruct((half_ff, D), BF16),
            ],
        )
    else:
        gather = partial(lax.all_gather, axis_name="fsdp", axis=0, tiled=True)
        first_full = gather(first_shard)
        projection_full = first_full[:, :split]
        output_full = first_full[:, split : split + D]
        vector_full = first_full[:, split + D :]
        expand_full = gather(expand_half)
        contract_full = gather(contract_half)

    vector_rows = f32(vector_full).T
    bias_parts = vector_rows[VECS : VECS + 3].reshape(3, shards, depth)
    projection_shift = lax.dynamic_index_in_dim(
        bias_parts.transpose(1, 0, 2).reshape(3, 2, half_d), side, 1, keepdims=False
    ).reshape(1, 3 * half_d)
    expand_parts = lax.dynamic_slice_in_dim(vector_rows, VECS + 3 + 2 * side, 2, 0)
    expand_shift = expand_parts.reshape(2, shards, depth).transpose(1, 0, 2).reshape(1, half_ff)
    output_half = lax.dynamic_slice_in_dim(output_full, side * half_d, half_d, 0)
    gain_one, gain_two = vector_rows[0], vector_rows[2]

    row_numbers = jnp.arange(rows_local, dtype=jnp.int32)
    positions = jnp.concatenate(
        [side * rows_local + row_numbers, (1 - side) * rows_local + row_numbers]
    )
    tables = rotary_lanes(positions)
    packed, hidden_one, hidden_two = project(
        token_rows, vector_rows[:8], projection_full, projection_shift, tables
    )
    context_grad = bf16(
        jnp.einsum("sf,df->sd", upstream, output_half, preferred_element_type=F32)
    )
    context, joint_grad = attention(
        side.astype(jnp.int32).reshape(1), packed, context_grad, tables
    )

    def dot_rows(left, right):
        return jnp.einsum("sd,sf->df", left, right, preferred_element_type=F32)

    grad_joint = jnp.einsum(
        "sd,csf->dcf", hidden_one, joint_grad, preferred_element_type=F32
    ).reshape(D, split)
    grad_output_half = dot_rows(context, upstream)
    hidden_one_grad = jnp.einsum(
        "csf,dcf->sd",
        joint_grad,
        projection_full.reshape(D, 3, half_d),
        preferred_element_type=F32,
    )
    attended = jnp.dot(context, output_half, preferred_element_type=F32)

    expanded = jnp.dot(hidden_two, expand_full, preferred_element_type=F32) + expand_shift
    activated, gelu_pull = jax.vjp(partial(jax.nn.gelu, approximate=False), expanded)
    activated = bf16(activated)
    mixed = jnp.dot(activated, contract_full, preferred_element_type=F32)
    partial_out = attended + mixed
    arrived_out = side_swap(bf16(partial_out[rows_local:]))
    grad_contract = dot_rows(activated, upstream)
    activated_grad = jnp.einsum("sf,hf->sh", upstream, contract_full, preferred_element_type=F32)
    (expanded_grad,) = gelu_pull(activated_grad)
    expanded_grad = bf16(expanded_grad)
    hidden_two_grad = jnp.einsum(
        "sh,dh->sd", expanded_grad, expand_full, preferred_element_type=F32
    )
    grad_expand = dot_rows(hidden_two, expanded_grad)

    layer_output = bf16(
        f32(own_tokens) + partial_out[:rows_local] + f32(arrived_out) + vector_rows[4] + vector_rows[5]
    )[None]

    values = f32(token_rows)
    average = jnp.mean(values, axis=-1, keepdims=True)
    centred = values - average
    scale = lax.rsqrt(jnp.mean(centred * centred, axis=-1, keepdims=True) + EPSILON)
    unit = centred * scale
    scaled = hidden_one_grad * gain_one + hidden_two_grad * gain_two
    pulled = (
        scaled
        - jnp.mean(scaled, axis=-1, keepdims=True)
        - unit * jnp.mean(scaled * unit, axis=-1, keepdims=True)
    ) * scale
    arrived_pull = side_swap(bf16(pulled[rows_local:]))
    tokens_grad = (f32(own_up) + pulled[:rows_local] + f32(arrived_pull))[None]

    own_bias = jnp.sum(f32(own_up), axis=0)
    joint_bias = jnp.sum(f32(joint_grad), axis=1)
    here = (jnp.arange(2) == side).astype(F32)
    joint_bias_row = (joint_bias[:, None, :] * here[None, :, None]).reshape(shards, 3 * depth)
    expand_bias_row = (
        jnp.sum(f32(expanded_grad), axis=0).reshape(shards, 1, wide) * here[None, :, None]
    ).reshape(shards, 2 * wide)
    small = jnp.concatenate(
        [
            jnp.sum(hidden_one_grad * unit, axis=0).reshape(shards, depth),
            jnp.sum(hidden_one_grad, axis=0).reshape(shards, depth),
            jnp.sum(hidden_two_grad * unit, axis=0).reshape(shards, depth),
            jnp.sum(hidden_two_grad, axis=0).reshape(shards, depth),
            own_bias.reshape(shards, depth),
            joint_bias_row,
            expand_bias_row,
        ],
        1,
    )

    mask = ((jnp.arange(shards) // (shards // 2)) == side).astype(F32)[:, None, None]
    output_blocks = jnp.tile(grad_output_half.reshape(shards // 2, depth, D), (2, 1, 1)) * mask
    if ring:
        first = jnp.concatenate([grad_joint.reshape(shards, depth, split), output_blocks], 2)
        core = me % 2
        first = ring_scatter(first, core, order, 1)
        joint_half, output_part = first[:, :split], first[:, split:]
        contract_part = ring_scatter(grad_contract.reshape(shards, wide, D), core, order, 0)
        expand_part = ring_scatter(grad_expand.reshape(shards, depth, half_ff), core, order, 1)
        small_part = small_ring(small, core, order)
    else:
        scatter = partial(lax.psum_scatter, axis_name="fsdp", scatter_dimension=0, tiled=False)
        joint_half = scatter(grad_joint.reshape(shards, depth, split))
        output_part = scatter(output_blocks)
        contract_part = scatter(grad_contract.reshape(shards, wide, D))
        expand_part = scatter(grad_expand.reshape(shards, depth, half_ff))
        small_part = scatter(small)

    joint_peer = f32(side_swap(bf16(joint_half)))
    output_grad = output_part + f32(side_swap(bf16(output_part)))
    contract_peer = f32(side_swap(bf16(contract_part)))
    expand_peer = f32(side_swap(bf16(expand_part)))
    small_sum = small_part + side_swap(small_part)

    def interleave(mine, peer, axis):
        first = jnp.where(side == 0, mine, peer)
        second = jnp.where(side == 0, peer, mine)
        return jnp.stack([first, second], axis)

    joint_grad_out = interleave(
        joint_half.reshape(depth, 3, half_d), joint_peer.reshape(depth, 3, half_d), 2
    ).reshape(depth, 3 * D)
    expand_grad_out = interleave(
        expand_part.reshape(depth, shards, wide), expand_peer.reshape(depth, shards, wide), 2
    ).reshape(depth, FF)
    contract_grad_out = interleave(contract_part, contract_peer, 0).reshape(2 * wide, D)
    pieces = [small_sum[depth * i : depth * (i + 1)] for i in range(5)]
    joint_bias_out = small_sum[5 * depth : 8 * depth]
    expand_bias_out = small_sum[8 * depth :]
    return (
        layer_output,
        tokens_grad,
        pieces[0],
        pieces[1],
        pieces[2],
        pieces[3],
        joint_grad_out,
        joint_bias_out,
        output_grad,
        pieces[4],
        expand_grad_out,
        expand_bias_out,
        contract_grad_out,
        pieces[4],
    )


def small_ring(small, core, order):
    by_core = small.reshape(8, 2, -1)
    mine = lax.dynamic_index_in_dim(by_core, core, 1, keepdims=False)
    other = lax.dynamic_index_in_dim(by_core, 1 - core, 1, keepdims=False)
    summed = mine + core_swap(other)

    def own(distance):
        return lax.dynamic_slice_in_dim(summed, order[distance] // 2, 1, 0)

    right = clockwise(own(4))
    right, left = own(3) + right, own(5)
    right, left = clockwise(right), counter(left)
    right, left = own(2) + right, own(6) + left
    right, left = clockwise(right), counter(left)
    right, left = own(1) + right, own(7) + left
    right, left = clockwise(right), counter(left)
    return (own(0) + right + left)[0]


def solution(mesh):
    return jax.shard_map(
        body,
        mesh=mesh,
        in_specs=(
            P("fsdp", "seq", None),
            P("fsdp"),
            P("fsdp"),
            P("fsdp"),
            P("fsdp"),
            P("fsdp", None),
            P("fsdp"),
            P("fsdp", None),
            P("fsdp"),
            P("fsdp", None),
            P("fsdp"),
            P("fsdp", None),
            P("fsdp"),
            P("fsdp", "seq", None),
        ),
        out_specs=(
            P("fsdp", "seq", None),
            P("fsdp", "seq", None),
            P("fsdp"),
            P("fsdp"),
            P("fsdp"),
            P("fsdp"),
            P("fsdp", None),
            P("fsdp"),
            P("fsdp", None),
            P("fsdp"),
            P("fsdp", None),
            P("fsdp"),
            P("fsdp", None),
            P("fsdp"),
        ),
        check_vma=False,
    )
```

```python
from functools import partial

import jax
import jax.numpy as jnp
import numpy as np
from jax import lax
from jax.experimental import pallas as pl
from jax.experimental.pallas import tpu as pltpu
from jax.sharding import PartitionSpec as P

D = 768
HD = 64
FF = 3072
ROT = 16
EPSILON = 1e-05
LANES = 128
ROWS = 256
PARAMS = pltpu.CompilerParams(vmem_limit_bytes=24 << 20)

F32 = jnp.float32
BF16 = jnp.bfloat16


def f32(value):
    return value.astype(F32)


def bf16(value):
    return value.astype(BF16)


RING_CHIPS = (0, 2, 4, 6, 7, 5, 3, 1)
RING_SIZE = 16


def ring_pairs(step):
    count = len(RING_CHIPS)
    return [
        (RING_CHIPS[i] * 2 + core, RING_CHIPS[(i + step) % count] * 2 + core)
        for i in range(count)
        for core in range(2)
    ]


CLOCKWISE = ring_pairs(1)
COUNTER = ring_pairs(-1)
CORE_SWAP = [(f, f ^ 1) for f in range(RING_SIZE)]
SIDE_SWAP = [(0, 1), (1, 0)]


def ring_table():
    table = np.zeros((RING_SIZE, 16), np.int32)
    for f in range(RING_SIZE):
        place = RING_CHIPS.index(f // 2)
        for distance in range(8):
            chip = RING_CHIPS[(place + distance) % 8]
            table[f, distance] = chip * 2 + f % 2
            table[f, 8 + distance] = chip * 2 + 1 - f % 2
    return table


def clockwise(value):
    return lax.ppermute(value, "fsdp", CLOCKWISE)


def counter(value):
    return lax.ppermute(value, "fsdp", COUNTER)


def core_swap(value):
    return lax.ppermute(value, "fsdp", CORE_SWAP)


def side_swap(value):
    return lax.ppermute(value, "seq", SIDE_SWAP)


PIECE_DISTANCES = (0, 1, 7, 2, 6, 3, 5, 4, 4)
PIECE_PARTS = ("all",) * 7 + ("a", "b")


def ring_gather(shard, split_axis, half):
    size = shard.shape[split_axis]
    right, left = shard, shard
    own, other = [shard], [core_swap(shard)]
    for step in range(1, 5):
        if step < 4:
            left, right = counter(left), clockwise(right)
            fresh = [left, right]
        else:
            fresh = [
                clockwise(lax.slice_in_dim(right, 0, half, axis=split_axis)),
                counter(lax.slice_in_dim(left, half, size, axis=split_axis)),
            ]
        own += fresh
        other += [core_swap(piece) for piece in fresh]
    return own + other


def piece_copies(meta_ref, pieces, outs, sem, copies_of):
    copies = []
    for number, piece in enumerate(pieces):
        core, place = divmod(number, 9)
        device = meta_ref[core * 8 + PIECE_DISTANCES[place]]
        for source, out, target in copies_of(PIECE_PARTS[place], device):
            copies.append(
                pltpu.make_async_copy(
                    piece.at[source], outs[out].at[target], sem.at[len(copies)]
                )
            )
    return copies


def copies_number(copies_of):
    return 2 * sum(len(copies_of(part, 0)) for part in PIECE_PARTS)


def device_rows(device, size):
    return pl.ds(device * size if isinstance(device, int) else pl.multiple_of(device * size, size), size)


def ring_scatter(keep, sent, axis, half):
    arrived = core_swap(sent)

    def own(distance):
        return f32(keep[distance]) + f32(arrived[distance])

    size = keep.shape[1 + axis]
    head = partial(lax.slice_in_dim, start_index=0, limit_index=half, axis=axis)
    tail = partial(lax.slice_in_dim, start_index=half, limit_index=size, axis=axis)
    far = own(4)
    right, left = bf16(head(far)), bf16(tail(far))
    right, left = clockwise(right), counter(left)
    near, back = own(3), own(5)
    right = bf16(jnp.concatenate([head(near) + f32(right), tail(near)], axis))
    left = bf16(jnp.concatenate([head(back), tail(back) + f32(left)], axis))
    right, left = clockwise(right), counter(left)
    right, left = bf16(own(2) + f32(right)), bf16(own(6) + f32(left))
    right, left = clockwise(right), counter(left)
    right, left = bf16(own(1) + f32(right)), bf16(own(7) + f32(left))
    right, left = clockwise(right), counter(left)
    return own(0) + f32(right) + f32(left)


TILE_ROWS = 24


def pack_kernel(side_ref, weight_ref, output_ref, *refs):
    vectors, three, four, out_ref, tile = refs[:6], refs[6], refs[7], refs[8], refs[9]
    half_d = D // 2
    for part in range(3):
        start = pl.multiple_of(part * D + side_ref[0] * half_d, LANES)
        out_ref[:, part * half_d : (part + 1) * half_d] = weight_ref[:, pl.ds(start, half_d)]
    out_ref[:, 3 * half_d : 3 * half_d + D] = output_ref[...]
    depth = weight_ref.shape[0]
    wide = four.shape[1] // 2
    tile[...] = jnp.zeros_like(tile)
    for row in range(6):
        tile[row : row + 1, :depth] = f32(vectors[row][...])
    shift = f32(three[...])
    tile[8:9, :] = shift[:, :LANES]
    tile[9:10, : 3 * depth - LANES] = shift[:, LANES:]
    tile[16:17, :wide] = f32(four[:, :wide])
    tile[17:18, :wide] = f32(four[:, wide:])
    out_ref[:, 3 * half_d + D :] = bf16(tile[...])


def pack(side, weight, output, vectors, three, four):
    depth = weight.shape[0]
    columns = 3 * D // 2 + D + LANES
    whole = pl.BlockSpec(memory_space=pltpu.VMEM)
    return pl.pallas_call(
        pack_kernel,
        grid_spec=pltpu.PrefetchScalarGridSpec(
            num_scalar_prefetch=1,
            grid=(),
            in_specs=[whole] * 10,
            out_specs=whole,
            scratch_shapes=[pltpu.VMEM((depth, LANES), F32)],
        ),
        out_shape=jax.ShapeDtypeStruct((depth, columns), BF16),
        compiler_params=PARAMS,
        name="pack",
    )(side, weight, output, *[v.reshape(1, -1) for v in vectors], three.reshape(1, -1), four.reshape(1, -1))


def unpack_tiles(tiles_ref, vec_ref, depth, wide):
    vec_ref[...] = jnp.zeros_like(vec_ref)
    for device in range(D // depth):
        tile = f32(tiles_ref[device * depth : device * depth + TILE_ROWS, :])
        columns = slice(device * depth, (device + 1) * depth)
        vec_ref[0:4, columns] = tile[0:4, :depth]
        vec_ref[4:5, columns] = tile[4:5, :depth] + tile[5:6, :depth]
        first = device * 3 * depth
        vec_ref[5:6, first : first + LANES] = tile[8:9, :]
        vec_ref[5:6, first + LANES : first + 3 * depth] = tile[9:10, : 3 * depth - LANES]
        vec_ref[6:8, device * wide : (device + 1) * wide] = tile[16:18, :wide]


def collect(side, first_ref, second_ref, third_ref, out):
    out[...] = jnp.zeros_like(out)
    out[0:2, :D] = first_ref[0:2, :D]
    out[2:4, :D] = second_ref[0:2, :D] + third_ref[0:2, :D]
    out[4:5, :D] = first_ref[5:6, :D]
    half = D // 2
    for part in range(3):
        start = pl.multiple_of(part * D + side * half, LANES)
        out[5:6, pl.ds(start, half)] = first_ref[2 + part : 3 + part, :half]
    expand = second_ref[2:3, :] + third_ref[2:3, :]
    wide = expand.shape[1]
    here = side == 0
    out[6:7, :wide] = jnp.where(here, expand, 0.0)
    out[7:8, :wide] = jnp.where(here, 0.0, expand)


def collect_kernel(meta_ref, first_ref, second_ref, third_ref, out):
    collect(meta_ref[16], first_ref, second_ref, third_ref, out)


def collect_sums(meta, first, second, third):
    whole = pl.BlockSpec(memory_space=pltpu.VMEM)
    return pl.pallas_call(
        collect_kernel,
        grid_spec=pltpu.PrefetchScalarGridSpec(
            num_scalar_prefetch=1, grid=(), in_specs=[whole] * 3, out_specs=whole
        ),
        out_shape=jax.ShapeDtypeStruct((8, 3 * D), F32),
        compiler_params=PARAMS,
        name="collect_sums",
    )(meta, first, second, third)


def pick_kernel(tile_ref, *outs):
    depth = outs[0].shape[1]
    wide = outs[6].shape[1] // 2
    for row in range(5):
        outs[row][...] = tile_ref[row : row + 1, :depth]
    outs[5][:, :LANES] = tile_ref[8:9, :]
    outs[5][:, LANES:] = tile_ref[9:10, : 3 * depth - LANES]
    outs[6][:, :wide] = tile_ref[16:17, :wide]
    outs[6][:, wide:] = tile_ref[17:18, :wide]


def pick_vectors(tile, depth, wide):
    sizes = [depth] * 5 + [3 * depth, 2 * wide]
    whole = pl.BlockSpec(memory_space=pltpu.VMEM)
    outs = pl.pallas_call(
        pick_kernel,
        in_specs=[whole],
        out_specs=[whole] * 7,
        out_shape=[jax.ShapeDtypeStruct((1, size), F32) for size in sizes],
        compiler_params=PARAMS,
        name="pick_vectors",
    )(tile)
    return [out.reshape(-1) for out in outs]


def unit_of(values):
    average = jnp.mean(values, axis=-1, keepdims=True)
    centred = values - average
    variance = jnp.mean(centred * centred, axis=-1, keepdims=True)
    scale = lax.rsqrt(variance + EPSILON)
    return centred * scale, scale


def project_rows(tokens, vec_ref, bias, weight, tables_ref, packed_ref, one_ref, two_ref):
    unit, _ = unit_of(f32(tokens))
    one = bf16(unit * vec_ref[0:1, :D] + vec_ref[1:2, :D])
    one_ref[...] = one
    two_ref[...] = bf16(unit * vec_ref[2:3, :D] + vec_ref[3:4, :D])
    projected = jnp.dot(one, weight, preferred_element_type=F32) + bias
    columns = projected.shape[1]
    cosine, plus, minus = tables_ref[0], tables_ref[1], tables_ref[2]
    for low in range(0, columns, LANES):
        piece = projected[:, low : low + LANES]
        if low < columns * 2 // 3:
            piece = (
                piece * cosine
                + pltpu.roll(piece, LANES - 8, 1) * plus
                + pltpu.roll(piece, 8, 1) * minus
            )
        packed_ref[:, low : low + LANES] = bf16(piece)


def project_kernel(copies_of, count, meta_ref, own_ref, peer_ref, tables_ref, *refs):
    pieces, rest = refs[:count], refs[count:]
    packed_ref, one_ref, two_ref, weight_ref, output_ref, vec_ref = rest[:6]
    step = pl.program_id(0)
    half_d = D // 2
    if copies_of is None:
        @pl.when(step == 0)
        def _():
            weight_ref[...] = pieces[0][:, : 3 * half_d]
            rows = pl.multiple_of(meta_ref[16] * half_d, half_d)
            output_ref[...] = pieces[0][pl.ds(rows, half_d), 3 * half_d :]
            vec_ref[...] = pieces[1][...]
    else:
        all_ref, tiles_ref, sem = rest[6:]

        @pl.when(step == 0)
        def _():
            outs = (weight_ref, all_ref, tiles_ref)
            copies = piece_copies(meta_ref, pieces, outs, sem, copies_of)
            for copy in copies:
                copy.start()
            for copy in copies:
                copy.wait()
            rows = pl.multiple_of(meta_ref[16] * half_d, half_d)
            output_ref[...] = all_ref[pl.ds(rows, half_d), :]
            shards = count * 8 // 9
            unpack_tiles(tiles_ref, vec_ref, D // shards, FF // shards // 2)

    blocks = own_ref.shape[0] // ROWS
    side = meta_ref[16]
    bias = jnp.concatenate(
        [
            vec_ref[5:6, pl.ds(pl.multiple_of(part * D + side * half_d, LANES), half_d)]
            for part in range(3)
        ],
        1,
    )
    rows = pl.ds(pl.multiple_of(lax.rem(step, blocks) * ROWS, ROWS), ROWS)
    tokens = jnp.where(step < blocks, own_ref[rows, :], peer_ref[rows, :])
    project_rows(tokens, vec_ref, bias, weight_ref[...], tables_ref, packed_ref, one_ref, two_ref)


def project(meta, own, peer, tables, pieces, copies_of):
    rows = 2 * own.shape[0]
    columns = 3 * D // 2
    count = len(pieces)
    scratch = []
    piece_spec = pl.BlockSpec(memory_space=pltpu.VMEM)
    if copies_of is not None:
        scratch = [
            pltpu.VMEM((D, D), BF16),
            pltpu.VMEM((D, LANES), BF16),
            pltpu.SemaphoreType.DMA((copies_number(copies_of),)),
        ]
        piece_spec = pl.BlockSpec(memory_space=pl.ANY)
    whole = lambda i, m: (0, 0)
    return pl.pallas_call(
        partial(project_kernel, copies_of, count),
        grid_spec=pltpu.PrefetchScalarGridSpec(
            num_scalar_prefetch=1,
            grid=(rows // ROWS,),
            in_specs=[
                pl.BlockSpec((rows // 2, D), whole),
                pl.BlockSpec((rows // 2, D), whole),
                pl.BlockSpec((3, ROWS, LANES), lambda i, m: (0, i, 0)),
            ]
            + [piece_spec] * count,
            out_specs=[
                pl.BlockSpec((ROWS, columns), lambda i, m: (i, 0)),
                pl.BlockSpec((ROWS, D), lambda i, m: (i, 0)),
                pl.BlockSpec((ROWS, D), lambda i, m: (i, 0)),
                pl.BlockSpec((D, columns), whole),
                pl.BlockSpec((D // 2, D), whole),
                pl.BlockSpec((8, 3 * D), whole),
            ],
            scratch_shapes=scratch,
        ),
        out_shape=[
            jax.ShapeDtypeStruct((rows, columns), BF16),
            jax.ShapeDtypeStruct((rows, D), BF16),
            jax.ShapeDtypeStruct((rows, D), BF16),
            jax.ShapeDtypeStruct((D, columns), BF16),
            jax.ShapeDtypeStruct((D // 2, D), BF16),
            jax.ShapeDtypeStruct((8, 3 * D), F32),
        ],
        compiler_params=PARAMS,
        name="project",
    )(meta, own, peer, tables, *pieces)


def rotary_lanes(positions):
    lane = jnp.arange(LANES, dtype=jnp.int32) % HD
    half = ROT // 2
    frequency = 10000.0 ** (-(2.0 * f32(lane % half)) / ROT)
    angles = f32(positions)[:, None] * frequency[None, :]
    cosine, sine = jnp.cos(angles), jnp.sin(angles)
    low = (lane < half)[None, :]
    high = ((lane >= half) & (lane < ROT))[None, :]
    return jnp.stack(
        [
            jnp.where(low | high, cosine, 1.0),
            jnp.where(low, -sine, 0.0),
            jnp.where(high, sine, 0.0),
        ]
    )


CONTRACT_ROWS = (((0,), (0,)), ((), ()))
CONTRACT_LAST = (((1,), (1,)), ((), ()))


def dot_rows(left, right):
    return lax.dot_general(left, right, CONTRACT_ROWS, preferred_element_type=F32)


def dot_last(left, right):
    return lax.dot_general(left, right, CONTRACT_LAST, preferred_element_type=F32)


def spread(meta_ref, total_ref, keep_ref, sent_ref):
    count, rows = keep_ref.shape[0], keep_ref.shape[1]
    for distance in range(count):
        if sent_ref is None:
            keep_ref[distance] = total_ref[distance * rows : (distance + 1) * rows, :]
        else:
            near = pl.multiple_of(meta_ref[distance] * rows, rows)
            keep_ref[distance] = total_ref[pl.ds(near, rows), :]
            far = pl.multiple_of(meta_ref[8 + distance] * rows, rows)
            sent_ref[distance] = bf16(total_ref[pl.ds(far, rows), :])


def grads_out(columns, block, depth, shards, ring):
    count = 8 if ring else shards
    specs = [pl.BlockSpec((count, depth, block), lambda i, m: (0, 0, i))]
    shapes = [jax.ShapeDtypeStruct((count, depth, columns), F32)]
    if ring:
        specs.append(pl.BlockSpec((count, depth, block), lambda i, m: (0, 0, i)))
        shapes.append(jax.ShapeDtypeStruct((count, depth, columns), BF16))
    return specs, shapes


def joint_grads_kernel(ring, meta_ref, one_ref, grads_ref, context_ref, own_ref, peer_ref, *refs):
    keep_ref, sent_ref, total_ref = refs[0], refs[1] if ring else None, refs[-1]
    step = pl.program_id(0)
    half_d = D // 2
    half = own_ref.shape[0]

    @pl.when(step < 3)
    def _():
        total_ref[...] = dot_rows(one_ref[...], grads_ref[0])

    @pl.when(step >= 3)
    def _():
        side = meta_ref[16]
        here = pl.ds(pl.multiple_of(side * half_d, half_d), half_d)
        there = pl.ds(pl.multiple_of((1 - side) * half_d, half_d), half_d)
        total_ref[there, :] = jnp.zeros((half_d, total_ref.shape[1]), F32)
        total_ref[here, :] = dot_rows(context_ref[:half], own_ref[...]) + dot_rows(
            context_ref[half:], peer_ref[...]
        )

    spread(meta_ref, total_ref, keep_ref, sent_ref)


def joint_grads(meta, one, grads, context, own, peer, depth, shards, ring):
    rows = one.shape[0]
    half_d = D // 2
    specs, shapes = grads_out(5 * half_d, half_d, depth, shards, ring)
    whole = lambda i, m: (0, 0)
    late = lambda i, m: (0, jnp.maximum(i - 3, 0))
    return pl.pallas_call(
        partial(joint_grads_kernel, ring),
        grid_spec=pltpu.PrefetchScalarGridSpec(
            num_scalar_prefetch=1,
            grid=(5,),
            in_specs=[
                pl.BlockSpec((rows, D), whole),
                pl.BlockSpec((1, rows, half_d), lambda i, m: (jnp.minimum(i, 2), 0, 0)),
                pl.BlockSpec((rows, half_d), whole),
                pl.BlockSpec((rows // 2, half_d), late),
                pl.BlockSpec((rows // 2, half_d), late),
            ],
            out_specs=specs,
            scratch_shapes=[pltpu.VMEM((D, half_d), F32)],
        ),
        out_shape=shapes,
        compiler_params=PARAMS,
        name="joint_grads",
    )(meta, one, grads, context, own, peer)


def joint_back_kernel(
    tokens_own_ref, tokens_peer_ref, up_ref, grads_ref, context_ref, weight_ref, output_ref,
    vec_ref, scaled_ref, attended_ref, sums_ref
):
    step = pl.program_id(0)
    half_d = D // 2
    blocks = tokens_own_ref.shape[0] // ROWS
    rows = pl.ds(pl.multiple_of(lax.rem(step, blocks) * ROWS, ROWS), ROWS)
    tokens = jnp.where(step < blocks, tokens_own_ref[rows, :], tokens_peer_ref[rows, :])
    unit, _ = unit_of(f32(tokens))
    total = dot_last(grads_ref[0], weight_ref[:, :half_d])
    for part in (1, 2):
        total = total + dot_last(
            grads_ref[part], weight_ref[:, part * half_d : (part + 1) * half_d]
        )
    scaled_ref[...] = total * vec_ref[0:1, :D]
    attended_ref[...] = jnp.dot(context_ref[...], output_ref[...], preferred_element_type=F32)

    @pl.when(step == 0)
    def _():
        sums_ref[...] = jnp.zeros_like(sums_ref)

    sums_ref[0:1, :] += jnp.sum(total * unit, axis=0, keepdims=True)
    sums_ref[1:2, :] += jnp.sum(total, axis=0, keepdims=True)
    for part in range(3):
        sums_ref[2 + part : 3 + part, :half_d] += jnp.sum(
            f32(grads_ref[part]), axis=0, keepdims=True
        )

    @pl.when(step < blocks)
    def _():
        sums_ref[5:6, :] += jnp.sum(f32(up_ref[rows, :]), axis=0, keepdims=True)


def joint_back(own, peer, up, grads, context, weight, output, vecs):
    rows = context.shape[0]
    half_d = D // 2
    whole = lambda i: (0, 0)
    return pl.pallas_call(
        joint_back_kernel,
        grid=(rows // ROWS,),
        in_specs=[
            pl.BlockSpec((rows // 2, D), whole),
            pl.BlockSpec((rows // 2, D), whole),
            pl.BlockSpec((rows // 2, D), whole),
            pl.BlockSpec((3, ROWS, half_d), lambda i: (0, i, 0)),
            pl.BlockSpec((ROWS, half_d), lambda i: (i, 0)),
            pl.BlockSpec((D, 3 * half_d), whole),
            pl.BlockSpec((half_d, D), whole),
            pl.BlockSpec((8, 3 * D), whole),
        ],
        out_specs=[
            pl.BlockSpec((ROWS, D), lambda i: (i, 0)),
            pl.BlockSpec((ROWS, D), lambda i: (i, 0)),
            pl.BlockSpec((8, D), whole),
        ],
        out_shape=[
            jax.ShapeDtypeStruct((rows, D), F32),
            jax.ShapeDtypeStruct((rows, D), F32),
            jax.ShapeDtypeStruct((8, D), F32),
        ],
        compiler_params=PARAMS,
        name="joint_back",
    )(own, peer, up, grads, context, weight, output, vecs)


def gelu_parts(v):
    phi = 0.5 * (1.0 + lax.erf(v * np.float32(np.sqrt(0.5))))
    density = jnp.exp(-0.5 * v * v) * np.float32(1.0 / np.sqrt(2.0 * np.pi))
    return v * phi, phi + v * density


def forward_kernel(copies_of, count, meta_ref, two_ref, attended_ref, vec_ref, *refs):
    pieces, rest = refs[:count], refs[count:]
    act_ref, slope_ref, out_ref = rest[:3]
    if copies_of is None:
        expand_ref, contract_ref = pieces
    else:
        expand_ref, contract_ref, sem = rest[3:6]

        @pl.when(pl.program_id(0) == 0)
        def _():
            copies = piece_copies(meta_ref, pieces, (expand_ref, contract_ref), sem, copies_of)
            for copy in copies:
                copy.start()
            for copy in copies:
                copy.wait()

    shift = jnp.where(meta_ref[16] == 0, vec_ref[6:7, : FF // 2], vec_ref[7:8, : FF // 2])
    expanded = jnp.dot(two_ref[...], expand_ref[...], preferred_element_type=F32) + shift
    activated, slope = gelu_parts(expanded)
    slope_ref[...] = slope
    activated = bf16(activated)
    act_ref[...] = activated
    mixed = jnp.dot(activated, contract_ref[...], preferred_element_type=F32)
    out_ref[...] = (attended_ref[...] + mixed).astype(out_ref.dtype)


def forward(meta, two, attended, vecs, pieces, copies_of, first, rows, out_type):
    half_ff = FF // 2
    count = len(pieces)
    whole = lambda i, m: (0, 0)
    scratch = []
    out_specs = [
        pl.BlockSpec((ROWS, half_ff), lambda i, m: (i, 0)),
        pl.BlockSpec((ROWS, half_ff), lambda i, m: (i, 0)),
        pl.BlockSpec((ROWS, D), lambda i, m: (i, 0)),
    ]
    out_shape = [
        jax.ShapeDtypeStruct((rows, half_ff), BF16),
        jax.ShapeDtypeStruct((rows, half_ff), F32),
        jax.ShapeDtypeStruct((rows, D), out_type),
    ]
    piece_specs = [
        pl.BlockSpec((D, half_ff), whole),
        pl.BlockSpec((half_ff, D), whole),
    ]
    if copies_of is not None:
        scratch = [pltpu.SemaphoreType.DMA((copies_number(copies_of),))]
        out_specs += piece_specs
        out_shape += [
            jax.ShapeDtypeStruct((D, half_ff), BF16),
            jax.ShapeDtypeStruct((half_ff, D), BF16),
        ]
        piece_specs = [pl.BlockSpec(memory_space=pl.ANY)] * count
    base = first // ROWS
    return pl.pallas_call(
        partial(forward_kernel, copies_of, count),
        grid_spec=pltpu.PrefetchScalarGridSpec(
            num_scalar_prefetch=1,
            grid=(rows // ROWS,),
            in_specs=[
                pl.BlockSpec((ROWS, D), lambda i, m: (base + i, 0)),
                pl.BlockSpec((ROWS, D), lambda i, m: (base + i, 0)),
                pl.BlockSpec((8, 3 * D), whole),
            ]
            + piece_specs,
            out_specs=out_specs,
            scratch_shapes=scratch,
        ),
        out_shape=out_shape,
        compiler_params=PARAMS,
        name="forward_peer" if first else "forward_own",
    )(meta, two, attended, vecs, *pieces)


def backward_kernel(
    own, tokens_ref, up_ref, slope_ref, scaled_ref, expand_ref, contract_ref, vec_ref,
    grad_ref, pulled_ref, sums_ref
):
    slope_grad = dot_last(up_ref[...], contract_ref[...])
    grad = bf16(slope_grad * slope_ref[...])
    grad_ref[...] = grad
    total = dot_last(grad, expand_ref[...])
    unit, scale = unit_of(f32(tokens_ref[...]))
    scaled = scaled_ref[...] + total * vec_ref[2:3, :D]
    pulled = (
        scaled
        - jnp.mean(scaled, axis=-1, keepdims=True)
        - unit * jnp.mean(scaled * unit, axis=-1, keepdims=True)
    ) * scale
    if own:
        pulled = pulled + f32(up_ref[...])
    pulled_ref[...] = pulled.astype(pulled_ref.dtype)

    @pl.when(pl.program_id(0) == 0)
    def _():
        sums_ref[...] = jnp.zeros_like(sums_ref)

    sums_ref[0:1, :D] += jnp.sum(total * unit, axis=0, keepdims=True)
    sums_ref[1:2, :D] += jnp.sum(total, axis=0, keepdims=True)
    sums_ref[2:3, :] += jnp.sum(f32(grad), axis=0, keepdims=True)


def backward(tokens, up, slope, scaled, expand, contract, vecs, own):
    rows = tokens.shape[0]
    half_ff = FF // 2
    base = 0 if own else rows // ROWS
    whole = lambda i: (0, 0)
    block = lambda i: (i, 0)
    return pl.pallas_call(
        partial(backward_kernel, own),
        grid=(rows // ROWS,),
        in_specs=[
            pl.BlockSpec((ROWS, D), block),
            pl.BlockSpec((ROWS, D), block),
            pl.BlockSpec((ROWS, half_ff), block),
            pl.BlockSpec((ROWS, D), lambda i: (base + i, 0)),
            pl.BlockSpec((D, half_ff), whole),
            pl.BlockSpec((half_ff, D), whole),
            pl.BlockSpec((8, 3 * D), whole),
        ],
        out_specs=[
            pl.BlockSpec((ROWS, half_ff), block),
            pl.BlockSpec((ROWS, D), block),
            pl.BlockSpec((8, half_ff), whole),
        ],
        out_shape=[
            jax.ShapeDtypeStruct((rows, half_ff), BF16),
            jax.ShapeDtypeStruct((rows, D), F32 if own else BF16),
            jax.ShapeDtypeStruct((8, half_ff), F32),
        ],
        compiler_params=PARAMS,
        name="backward_own" if own else "backward_peer",
    )(tokens, up, slope, scaled, expand, contract, vecs)


def weight_grads_kernel(ring, sums, meta_ref, left_own, left_peer, right_own, right_peer, *refs):
    parts, refs = refs[:sums], refs[sums:]
    keep_ref, sent_ref, total_ref = refs[0], refs[1] if ring else None, refs[2 if ring else 1]
    step = pl.program_id(0)

    def products():
        total_ref[...] = dot_rows(left_own[...], right_own[...]) + dot_rows(
            left_peer[...], right_peer[...]
        )

    if sums:
        vec_ref = refs[3]
        last = pl.num_programs(0) - 1
        pl.when(step < last)(products)

        @pl.when(step == last)
        def _():
            collect(meta_ref[16], *parts, vec_ref)
            depth = keep_ref.shape[1]
            width = vec_ref.shape[1]
            total_ref[...] = jnp.zeros_like(total_ref)
            values = vec_ref[...]
            for device in range(D // depth):

                def rolled(size):
                    shift = device * size
                    return pltpu.roll(values, width - shift, 1) if shift else values

                row = device * depth
                total_ref[row : row + 8, :LANES] = rolled(depth)[:, :LANES]
                bias = rolled(3 * depth)
                total_ref[row + 8 : row + 9, :LANES] = bias[5:6, :LANES]
                total_ref[row + 9 : row + 10, :LANES] = bias[5:6, LANES : 2 * LANES]
                total_ref[row + 16 : row + 18, :LANES] = rolled(2 * depth)[6:8, :LANES]

    else:
        products()
    spread(meta_ref, total_ref, keep_ref, sent_ref)


def weight_grads(meta, left, right, rows_each, shards, ring, sums=()):
    (left_own, left_peer, left_shift), (right_own, right_peer) = left, right
    rows = right_own.shape[0]
    depth = left_own.shape[1]
    block = 384
    steps = right_own.shape[1] // block
    columns = right_own.shape[1] + (block if sums else 0)
    specs, shapes = grads_out(columns, block, rows_each, shards, ring)
    column = lambda i, m: (0, jnp.minimum(i, steps - 1))
    scratch = [pltpu.VMEM((depth, block), F32)]
    if sums:
        scratch.append(pltpu.VMEM((8, 3 * D), F32))
    return pl.pallas_call(
        partial(weight_grads_kernel, ring, len(sums)),
        grid_spec=pltpu.PrefetchScalarGridSpec(
            num_scalar_prefetch=1,
            grid=(columns // block,),
            in_specs=[
                pl.BlockSpec((rows, depth), lambda i, m: (0, 0)),
                pl.BlockSpec((rows, depth), lambda i, m: (left_shift, 0)),
                pl.BlockSpec((rows, block), column),
                pl.BlockSpec((rows, block), column),
            ]
            + [pl.BlockSpec(part.shape, lambda i, m: (0, 0)) for part in sums],
            out_specs=specs,
            scratch_shapes=scratch,
        ),
        out_shape=shapes,
        compiler_params=PARAMS,
    )(meta, left_own, left_peer, right_own, right_peer, *sums)


def attention_kernel(
    side_ref, q_ref, k_ref, v_ref, own_ref, peer_ref, output_ref, tables_ref, context_ref,
    grads_ref, dk_acc, dv_acc
):
    rows = q_ref.shape[0]
    half = rows // 2
    block = min(256, half)
    start_one = pl.multiple_of(side_ref[16] * half, half)
    start_two = pl.multiple_of((1 - side_ref[16]) * half, half)

    def natural(ref):
        return jnp.concatenate([ref[pl.ds(start_one, half), :], ref[pl.ds(start_two, half), :]], 0)

    q = natural(q_ref) * jnp.asarray(0.125, BF16)
    k = natural(k_ref)
    v = natural(v_ref)
    up_own = bf16(dot_last(own_ref[...], output_ref[...]))
    up_peer = bf16(dot_last(peer_ref[...], output_ref[...]))
    second = side_ref[16] == 1
    up = jnp.concatenate(
        [jnp.where(second, up_peer, up_own), jnp.where(second, up_own, up_peer)], 0
    )
    lane = lax.broadcasted_iota(jnp.int32, (1, LANES), 1)
    contract_last = (((1,), (1,)), ((), ()))
    contract_first = (((0,), (0,)), ((), ()))
    dk_acc[...] = jnp.zeros_like(dk_acc)
    dv_acc[...] = jnp.zeros_like(dv_acc)
    below = lax.broadcasted_iota(jnp.int32, (block, block), 0) <= lax.broadcasted_iota(
        jnp.int32, (block, block), 1
    )

    def rotate_back(values, start):
        cosine = tables_ref[0, pl.ds(start, values.shape[0]), :]
        plus = tables_ref[1, pl.ds(start, values.shape[0]), :]
        minus = tables_ref[2, pl.ds(start, values.shape[0]), :]
        return (
            values * cosine
            - pltpu.roll(values, LANES - 8, 1) * plus
            - pltpu.roll(values, 8, 1) * minus
        )

    def local(row):
        return pl.multiple_of(
            (start_one if row < half else start_two) + (row if row < half else row - half), block
        )

    for number in range(rows // block):
        low, high = number * block, (number + 1) * block
        context_total = None
        dq_total = None
        for head in range(LANES // HD):
            mask = (lane // HD == head).astype(BF16)
            q_head = q[low:high] * mask
            up_head = up[low:high] * mask
            k_head = k[:high] * mask
            v_head = v[:high] * mask
            scores = lax.dot_general(k[:high], q_head, contract_last, preferred_element_type=F32)
            diagonal = jnp.where(below, scores[low:high], -1e30)
            scores = diagonal if low == 0 else jnp.concatenate([scores[:low], diagonal], 0)
            highest = jnp.max(scores, axis=0, keepdims=True)
            expo = jnp.exp(scores - highest)
            total = jnp.sum(expo, axis=0, keepdims=True)
            probs = expo * (1.0 / total)
            weights = probs.astype(BF16)
            weights_grad = lax.dot_general(
                v[:high], up_head, contract_last, preferred_element_type=F32
            )
            inner = jnp.sum(probs * weights_grad, axis=0, keepdims=True)
            scores_grad = (probs * (weights_grad - inner)).astype(BF16)
            context = lax.dot_general(
                v_head, weights, contract_first, preferred_element_type=F32
            )
            dq = lax.dot_general(k_head, scores_grad, contract_first, preferred_element_type=F32)
            context_total = context if context_total is None else context_total + context
            dq_total = dq if dq_total is None else dq_total + dq
            dv_acc[:high, :] += jnp.dot(weights, up_head, preferred_element_type=F32)
            dk_acc[:high, :] += jnp.dot(scores_grad, q_head, preferred_element_type=F32)
        place = local(low)
        context_ref[pl.ds(place, block), :] = context_total.T.astype(BF16)
        dq_low = (dq_total.T * 0.125).astype(BF16).astype(F32)
        grads_ref[0, pl.ds(place, block), :] = rotate_back(dq_low, place).astype(BF16)
    for number in range(rows // block):
        low = number * block
        place = local(low)
        dk_low = dk_acc[low : low + block, :].astype(BF16).astype(F32)
        grads_ref[1, pl.ds(place, block), :] = rotate_back(dk_low, place).astype(BF16)
        grads_ref[2, pl.ds(place, block), :] = dv_acc[low : low + block, :].astype(BF16)


def attention(side, packed, own, peer, output, tables):
    rows, columns = packed.shape[0], packed.shape[1] // 3
    pairs = columns // LANES
    return pl.pallas_call(
        attention_kernel,
        grid_spec=pltpu.PrefetchScalarGridSpec(
            num_scalar_prefetch=1,
            grid=(pairs,),
            in_specs=[
                pl.BlockSpec((rows, LANES), lambda i, s: (0, i)),
                pl.BlockSpec((rows, LANES), lambda i, s: (0, pairs + i)),
                pl.BlockSpec((rows, LANES), lambda i, s: (0, 2 * pairs + i)),
                pl.BlockSpec((rows // 2, D), lambda i, s: (0, 0)),
                pl.BlockSpec((rows // 2, D), lambda i, s: (0, 0)),
                pl.BlockSpec((LANES, D), lambda i, s: (i, 0)),
                pl.BlockSpec((3, rows, LANES), lambda i, s: (0, 0, 0)),
            ],
            out_specs=[
                pl.BlockSpec((rows, LANES), lambda i, s: (0, i)),
                pl.BlockSpec((3, rows, LANES), lambda i, s: (0, 0, i)),
            ],
            scratch_shapes=[pltpu.VMEM((rows, LANES), F32), pltpu.VMEM((rows, LANES), F32)],
        ),
        out_shape=[
            jax.ShapeDtypeStruct((rows, columns), BF16),
            jax.ShapeDtypeStruct((3, rows, columns), BF16),
        ],
        compiler_params=PARAMS,
        name="attention",
    )(side, packed, packed, packed, own, peer, output, tables)


def layer(
    tokens,
    first_norm_gain,
    first_norm_shift,
    second_norm_gain,
    second_norm_shift,
    projection_weight,
    projection_bias,
    output_weight,
    output_bias,
    expand_weight,
    expand_bias,
    contract_weight,
    contract_bias,
    cotangent,
):
    shards = lax.axis_size("fsdp")
    ring = shards == RING_SIZE
    me = lax.axis_index("fsdp").astype(jnp.int32)
    side = lax.axis_index("seq").astype(jnp.int32)
    rows = tokens.shape[1]
    depth = D // shards
    wide = FF // shards // 2
    half_d, half_ff = D // 2, FF // 2
    split = 3 * half_d
    here = side == 0

    own_tokens, own_up = tokens[0], cotangent[0]
    peer_tokens = side_swap(own_tokens)
    peer_up = side_swap(own_up)

    vectors = [
        first_norm_gain,
        first_norm_shift,
        second_norm_gain,
        second_norm_shift,
        output_bias,
        contract_bias,
    ]
    by_side = expand_weight.reshape(depth, shards, 2, wide)
    expand_half = jnp.where(here, by_side[:, :, 0], by_side[:, :, 1]).reshape(depth, half_ff)
    contract_half = jnp.where(here, contract_weight[:wide], contract_weight[wide:])
    first_copies = second_copies = None
    if ring:
        order = lax.dynamic_index_in_dim(jnp.asarray(ring_table()), me, 0, keepdims=False)
        meta = jnp.concatenate([order, side.reshape(1)])
        first_shard = pack(
            side.reshape(1), projection_weight, output_weight, vectors, projection_bias, expand_bias
        )
        second_shard = jnp.concatenate(
            [expand_half[:, :D], expand_half[:, D:], contract_half], 0
        )
        middle = 8 * LANES
        first_pieces = ring_gather(first_shard, 1, middle)
        second_pieces = ring_gather(second_shard, 0, 2 * depth)

        def first_copies(part, device):
            lines = device_rows(device, depth)
            every = pl.ds(0, depth)
            if part == "a":
                return [((every, pl.ds(0, middle)), 0, (lines, pl.ds(0, middle)))]
            shift = middle if part == "b" else 0
            return [
                ((every, pl.ds(0, split - shift)), 0, (lines, pl.ds(shift, split - shift))),
                ((every, pl.ds(split - shift, D)), 1, (lines, pl.ds(0, D))),
                ((every, pl.ds(split - shift + D, LANES)), 2, (lines, pl.ds(0, LANES))),
            ]

        def second_copies(part, device):
            lines = device_rows(device, depth)
            low = ((pl.ds(0, depth), pl.ds(0, D)), 0, (lines, pl.ds(0, D)))
            high = ((pl.ds(depth, depth), pl.ds(0, D)), 0, (lines, pl.ds(D, D)))
            start = 0 if part == "b" else 2 * depth
            last = ((pl.ds(start, wide), pl.ds(0, D)), 1, (device_rows(device, wide), pl.ds(0, D)))
            return {"all": [low, high, last], "a": [low, high], "b": [last]}[part]

    else:
        gather = partial(lax.all_gather, axis_name="fsdp", axis=0, tiled=True)
        meta = jnp.concatenate([jnp.zeros((16,), jnp.int32), side.reshape(1)])
        by_half = projection_weight.reshape(depth, 3, 2, half_d)
        projection_half = jnp.where(here, by_half[:, :, 0], by_half[:, :, 1])
        first_full = gather(
            jnp.concatenate([projection_half.reshape(depth, split), output_weight], 1)
        )
        gathered = [f32(gather(v)) for v in vectors]
        shift = gather(expand_bias).reshape(shards, 2, wide)
        vecs = jnp.zeros((8, 3 * D), F32)
        for row, value in enumerate(gathered[:4]):
            vecs = vecs.at[row, :D].set(value)
        vecs = vecs.at[4, :D].set(gathered[4] + gathered[5])
        vecs = vecs.at[5].set(f32(gather(projection_bias)))
        for part in range(2):
            vecs = vecs.at[6 + part, :half_ff].set(f32(shift[:, part].reshape(half_ff)))
        first_pieces = [first_full, vecs]
        second_pieces = [gather(expand_half), gather(contract_half)]

    row_numbers = jnp.arange(rows, dtype=jnp.int32)
    positions = jnp.concatenate([side * rows + row_numbers, (1 - side) * rows + row_numbers])
    tables = rotary_lanes(positions)
    packed, one, two, projection_full, output_half, vecs = project(
        meta, own_tokens, peer_tokens, tables, first_pieces, first_copies
    )
    context, grads = attention(meta, packed, own_up, peer_up, output_half, tables)

    def reduced(parts, axis, half):
        if ring:
            return ring_scatter(parts[0], parts[1], axis, half)
        return lax.psum_scatter(parts[0], "fsdp", scatter_dimension=0, tiled=False)

    joint_parts = list(
        joint_grads(meta, one, grads, context, own_up, peer_up, depth, shards, ring)
    )
    grads, joint_parts[-1] = lax.optimization_barrier((grads, joint_parts[-1]))
    first = reduced(joint_parts, 1, 8 * LANES)
    scaled, attended, sums_one = joint_back(
        own_tokens, peer_tokens, own_up, grads, context, projection_full, output_half, vecs
    )
    peer_parts = forward(
        meta, two, attended, vecs, second_pieces, second_copies, rows, rows, BF16
    )
    act_peer, slope_peer, out_peer = peer_parts[:3]
    expand_full, contract_full = peer_parts[3:] if ring else second_pieces
    out_arrived = side_swap(out_peer)
    act_own, slope_own, out_own = forward(
        meta, two, attended, vecs, [expand_full, contract_full], None, 0, rows, F32
    )
    contract_parts = list(
        weight_grads(meta, (act_own, act_peer, 0), (own_up, peer_up), wide, shards, ring)
    )
    slope_peer, contract_parts[-1] = lax.optimization_barrier((slope_peer, contract_parts[-1]))
    contract_part = reduced(contract_parts, 0, wide // 2)
    grad_peer, pulled_peer, sums_peer = backward(
        peer_tokens, peer_up, slope_peer, scaled, expand_full, contract_full, vecs, False
    )
    slope_own, pulled_peer = lax.optimization_barrier((slope_own, pulled_peer))
    pulled_arrived = side_swap(pulled_peer)
    grad_own, pulled_own, sums_own = backward(
        own_tokens, own_up, slope_own, scaled, expand_full, contract_full, vecs, True
    )
    sums = (sums_one, sums_peer, sums_own)
    expand_parts = weight_grads(
        meta, (two, two, 1), (grad_own, grad_peer), depth, shards, ring, sums if ring else ()
    )
    if ring:
        expand_parts = [part[:, :, : half_ff + LANES] for part in expand_parts]
    expand_part = reduced(expand_parts, 1, half_ff // 2)

    layer_output = bf16(f32(own_tokens) + out_own + f32(out_arrived) + vecs[4:5, :D])[None]
    tokens_grad = (pulled_own + f32(pulled_arrived))[None]

    def both(mine):
        peer = f32(side_swap(bf16(mine)))
        return jnp.where(here, mine, peer), jnp.where(here, peer, mine), mine + peer

    zero, one_side, total = both(first)
    joint_grad = jnp.stack(
        [zero[:, :split].reshape(depth, 3, half_d), one_side[:, :split].reshape(depth, 3, half_d)],
        2,
    ).reshape(depth, 3 * D)
    output_grad = total[:, split:]
    zero, one_side, _ = both(contract_part)
    contract_grad = jnp.concatenate([zero, one_side], 0)
    zero, one_side, total = both(expand_part)
    zero, one_side = zero[:, :half_ff], one_side[:, :half_ff]
    expand_grad = jnp.stack(
        [zero.reshape(depth, shards, wide), one_side.reshape(depth, shards, wide)], 2
    ).reshape(depth, FF)
    if ring:
        picked = pick_vectors(total[:, half_ff:], depth, wide)
    else:
        small = lax.psum(collect_sums(meta, *sums), ("fsdp", "seq"))

        def own_part(row, size):
            return lax.dynamic_slice(small, (row, me * size), (1, size))[0]

        picked = [own_part(row, depth) for row in range(5)]
        picked.append(own_part(5, 3 * depth))
        picked.append(jnp.concatenate([own_part(6, wide), own_part(7, wide)]))
    gain_one, shift_one, gain_two, shift_two, bias, joint_bias, expand_bias_grad = picked
    return (
        layer_output,
        tokens_grad,
        gain_one,
        shift_one,
        gain_two,
        shift_two,
        joint_grad,
        joint_bias,
        output_grad,
        bias,
        expand_grad,
        expand_bias_grad,
        contract_grad,
        bias,
    )


def solution(mesh):
    return jax.shard_map(
        layer,
        mesh=mesh,
        in_specs=(
            P("fsdp", "seq", None),
            P("fsdp"),
            P("fsdp"),
            P("fsdp"),
            P("fsdp"),
            P("fsdp", None),
            P("fsdp"),
            P("fsdp", None),
            P("fsdp"),
            P("fsdp", None),
            P("fsdp"),
            P("fsdp", None),
            P("fsdp"),
            P("fsdp", "seq", None),
        ),
        out_specs=(
            P("fsdp", "seq", None),
            P("fsdp", "seq", None),
            P("fsdp"),
            P("fsdp"),
            P("fsdp"),
            P("fsdp"),
            P("fsdp", None),
            P("fsdp"),
            P("fsdp", None),
            P("fsdp"),
            P("fsdp", None),
            P("fsdp"),
            P("fsdp", None),
            P("fsdp"),
        ),
        check_vma=False,
    )
```

```python
from functools import partial

import jax
import jax.numpy as jnp
import numpy as np
from jax import lax
from jax.experimental import pallas as pl
from jax.experimental.pallas import tpu as pltpu
from jax.sharding import PartitionSpec as P

D = 768
HD = 64
FF = 3072
ROT = 16
EPSILON = 1e-05
LANES = 128
ROWS = 256
PARAMS = pltpu.CompilerParams(vmem_limit_bytes=24 << 20)

F32 = jnp.float32
BF16 = jnp.bfloat16


def in_memory(space, values):
    return [pltpu.with_memory_space_constraint(value, space) for value in values]


def f32(value):
    return value.astype(F32)


def bf16(value):
    return value.astype(BF16)


RING_CHIPS = (0, 2, 4, 6, 7, 5, 3, 1)
RING_SIZE = 16


def ring_pairs(step):
    count = len(RING_CHIPS)
    return [
        (RING_CHIPS[i] * 2 + core, RING_CHIPS[(i + step) % count] * 2 + core)
        for i in range(count)
        for core in range(2)
    ]


CLOCKWISE = ring_pairs(1)
COUNTER = ring_pairs(-1)
CORE_SWAP = [(f, f ^ 1) for f in range(RING_SIZE)]
SIDE_SWAP = [(0, 1), (1, 0)]


def ring_table():
    table = np.zeros((RING_SIZE, 16), np.int32)
    for f in range(RING_SIZE):
        place = RING_CHIPS.index(f // 2)
        for distance in range(8):
            chip = RING_CHIPS[(place + distance) % 8]
            table[f, distance] = chip * 2 + f % 2
            table[f, 8 + distance] = chip * 2 + 1 - f % 2
    return table


def clockwise(value):
    return lax.ppermute(value, "fsdp", CLOCKWISE)


def counter(value):
    return lax.ppermute(value, "fsdp", COUNTER)


def core_swap(value):
    return lax.ppermute(value, "fsdp", CORE_SWAP)


def side_swap(value):
    return lax.ppermute(value, "seq", SIDE_SWAP)


PIECE_DISTANCES = (0, 1, 7, 2, 6, 3, 5, 4, 4)
PIECE_PARTS = ("all",) * 7 + ("a", "b")


def ring_gather(shard, split_axis, half):
    size = shard.shape[split_axis]
    right, left = shard, shard
    own, other = [shard], [core_swap(shard)]
    for step in range(1, 5):
        if step < 4:
            left, right = counter(left), clockwise(right)
            fresh = [left, right]
        else:
            fresh = [
                clockwise(lax.slice_in_dim(right, 0, half, axis=split_axis)),
                counter(lax.slice_in_dim(left, half, size, axis=split_axis)),
            ]
        own += fresh
        other += [core_swap(piece) for piece in fresh]
    return own + other


def piece_copies(meta_ref, pieces, outs, sem, copies_of):
    copies = []
    for number, piece in enumerate(pieces):
        core, place = divmod(number, 9)
        device = meta_ref[core * 8 + PIECE_DISTANCES[place]]
        for source, out, target in copies_of(PIECE_PARTS[place], device):
            copies.append(
                pltpu.make_async_copy(
                    piece.at[source], outs[out].at[target], sem.at[len(copies)]
                )
            )
    return copies


def copies_number(copies_of):
    return 2 * sum(len(copies_of(part, 0)) for part in PIECE_PARTS)


def device_rows(device, size):
    return pl.ds(device * size if isinstance(device, int) else pl.multiple_of(device * size, size), size)


def tick_kernel(kind, cut, *refs):
    if kind == "first":
        keep, other, right_out, left_out = refs
        total = keep[...] + f32(other[...])
        right_out[...] = bf16(total[:, :cut])
        left_out[...] = bf16(total[:, cut:])
    elif kind == "last":
        keep, other, right, left, total_out, low_out = refs
        total = keep[...] + f32(other[...]) + f32(right[...]) + f32(left[...])
        total_out[...] = total
        low_out[...] = bf16(total)
    else:
        keep_right, other_right, keep_left, other_left, right, left, right_out, left_out = refs
        total_right = keep_right[...] + f32(other_right[...])
        total_left = keep_left[...] + f32(other_left[...])
        if kind == "second":
            right_out[:, :cut] = bf16(total_right[:, :cut] + f32(right[...]))
            right_out[:, cut:] = bf16(total_right[:, cut:])
            left_out[:, :cut] = bf16(total_left[:, :cut])
            left_out[:, cut:] = bf16(total_left[:, cut:] + f32(left[...]))
        else:
            right_out[...] = bf16(total_right + f32(right[...]))
            left_out[...] = bf16(total_left + f32(left[...]))


def ring_scatter(keep, sent, cut):
    rows, columns = keep.shape[1:]
    arrived = core_swap(sent)

    def tick(kind, distances, moving, widths, types):
        ins, specs = [], []
        for distance in distances:
            for array in (keep, arrived):
                ins.append(array)
                specs.append(
                    pl.BlockSpec((None, rows, columns), lambda i, d=distance: (d, 0, 0))
                )
        for array in moving:
            ins.append(array)
            specs.append(pl.BlockSpec(array.shape, lambda i: (0, 0)))
        return pl.pallas_call(
            partial(tick_kernel, kind, cut),
            grid=(1,),
            in_specs=specs,
            out_specs=[pl.BlockSpec((rows, width), lambda i: (0, 0)) for width in widths],
            out_shape=[
                jax.ShapeDtypeStruct((rows, width), kept) for width, kept in zip(widths, types)
            ],
            compiler_params=PARAMS,
        )(*ins)

    def turn(right, left):
        return clockwise(right), counter(left)

    both, low = [columns] * 2, [BF16] * 2
    moving = turn(*tick("first", (4,), (), [cut, columns - cut], low))
    moving = turn(*tick("second", (3, 5), moving, both, low))
    moving = turn(*tick("middle", (2, 6), moving, both, low))
    moving = turn(*tick("middle", (1, 7), moving, both, low))
    return tick("last", (0,), moving, both, [F32, BF16])


TILE_ROWS = 24


def pack_kernel(side_ref, weight_ref, output_ref, flat_ref, out_ref, tile):
    half_d = D // 2
    for part in range(3):
        start = pl.multiple_of(part * D + side_ref[0] * half_d, LANES)
        out_ref[:, part * half_d : (part + 1) * half_d] = weight_ref[:, pl.ds(start, half_d)]
    out_ref[:, 3 * half_d : 3 * half_d + D] = output_ref[...]
    depth = weight_ref.shape[0]
    wide = 2 * depth
    flat = f32(flat_ref[...])
    tile[...] = jnp.zeros_like(tile)
    for row in range(6):
        tile[row : row + 1, :depth] = flat[:, row * depth : (row + 1) * depth]
    start = 6 * depth
    tile[8:9, :] = flat[:, start : start + LANES]
    tile[9:10, : 3 * depth - LANES] = flat[:, start + LANES : start + 3 * depth]
    start += 3 * depth
    for part in range(2):
        tile[16 + part : 17 + part, :wide] = flat[:, start : start + wide]
        start += wide
    out_ref[:, 3 * half_d + D :] = bf16(tile[...])


def pack(side, weight, output, flat):
    depth = weight.shape[0]
    columns = 3 * D // 2 + D + LANES
    whole = lambda i, s: (0, 0)
    return pl.pallas_call(
        pack_kernel,
        grid_spec=pltpu.PrefetchScalarGridSpec(
            num_scalar_prefetch=1,
            grid=(1,),
            in_specs=[
                pl.BlockSpec(weight.shape, whole),
                pl.BlockSpec(output.shape, whole),
                pl.BlockSpec(flat.shape, whole),
            ],
            out_specs=pl.BlockSpec((depth, columns), whole),
            scratch_shapes=[pltpu.VMEM((depth, LANES), F32)],
        ),
        out_shape=jax.ShapeDtypeStruct((depth, columns), BF16),
        compiler_params=PARAMS,
        name="pack",
    )(side, *in_memory(pltpu.HBM, [weight, output]), flat)


def unpack_tiles(tiles_ref, vec_ref, depth, wide):
    vec_ref[...] = jnp.zeros_like(vec_ref)
    for device in range(D // depth):
        tile = f32(tiles_ref[device * depth : device * depth + TILE_ROWS, :])
        columns = slice(device * depth, (device + 1) * depth)
        vec_ref[0:4, columns] = tile[0:4, :depth]
        vec_ref[4:5, columns] = tile[4:5, :depth] + tile[5:6, :depth]
        first = device * 3 * depth
        vec_ref[5:6, first : first + LANES] = tile[8:9, :]
        vec_ref[5:6, first + LANES : first + 3 * depth] = tile[9:10, : 3 * depth - LANES]
        vec_ref[6:8, device * wide : (device + 1) * wide] = tile[16:18, :wide]


def collect(side, first_ref, second_ref, third_ref, out):
    out[...] = jnp.zeros_like(out)
    out[0:2, :D] = first_ref[0:2, :D]
    out[2:4, :D] = second_ref[0:2, :D] + third_ref[0:2, :D]
    out[4:5, :D] = first_ref[5:6, :D]
    half = D // 2
    for part in range(3):
        start = pl.multiple_of(part * D + side * half, LANES)
        out[5:6, pl.ds(start, half)] = first_ref[2 + part : 3 + part, :half]
    expand = second_ref[2:3, :] + third_ref[2:3, :]
    wide = expand.shape[1]
    here = side == 0
    out[6:7, :wide] = jnp.where(here, expand, 0.0)
    out[7:8, :wide] = jnp.where(here, 0.0, expand)


def collect_kernel(meta_ref, first_ref, second_ref, third_ref, out):
    collect(meta_ref[16], first_ref, second_ref, third_ref, out)


def collect_sums(meta, first, second, third):
    whole = pl.BlockSpec(memory_space=pltpu.VMEM)
    return pl.pallas_call(
        collect_kernel,
        grid_spec=pltpu.PrefetchScalarGridSpec(
            num_scalar_prefetch=1, grid=(), in_specs=[whole] * 3, out_specs=whole
        ),
        out_shape=jax.ShapeDtypeStruct((8, 3 * D), F32),
        compiler_params=PARAMS,
        name="collect_sums",
    )(meta, first, second, third)


def unit_of(values):
    average = jnp.mean(values, axis=-1, keepdims=True)
    centred = values - average
    variance = jnp.mean(centred * centred, axis=-1, keepdims=True)
    scale = lax.rsqrt(variance + EPSILON)
    return centred * scale, scale


def project_rows(tokens, vec_ref, bias, weight, tables_ref, packed_ref, one_ref, two_ref):
    unit, _ = unit_of(f32(tokens))
    one = bf16(unit * vec_ref[0:1, :D] + vec_ref[1:2, :D])
    one_ref[...] = one
    two_ref[...] = bf16(unit * vec_ref[2:3, :D] + vec_ref[3:4, :D])
    projected = jnp.dot(one, weight, preferred_element_type=F32) + bias
    columns = projected.shape[1]
    cosine, plus, minus = tables_ref[0], tables_ref[1], tables_ref[2]
    for low in range(0, columns, LANES):
        piece = projected[:, low : low + LANES]
        if low < columns * 2 // 3:
            piece = (
                piece * cosine
                + pltpu.roll(piece, LANES - 8, 1) * plus
                + pltpu.roll(piece, 8, 1) * minus
            )
        packed_ref[:, low : low + LANES] = bf16(piece)


def project_kernel(copies_of, count, meta_ref, own_ref, peer_ref, tables_ref, *refs):
    pieces, rest = refs[:count], refs[count:]
    packed_ref, one_ref, two_ref, weight_ref, output_ref, vec_ref = rest[:6]
    step = pl.program_id(0)
    half_d = D // 2
    if copies_of is None:
        @pl.when(step == 0)
        def _():
            weight_ref[...] = pieces[0][:, : 3 * half_d]
            rows = pl.multiple_of(meta_ref[16] * half_d, half_d)
            output_ref[...] = pieces[0][pl.ds(rows, half_d), 3 * half_d :]
            vec_ref[...] = pieces[1][...]
    else:
        all_ref, tiles_ref, sem = rest[6:]

        @pl.when(step == 0)
        def _():
            outs = (weight_ref, all_ref, tiles_ref)
            copies = piece_copies(meta_ref, pieces, outs, sem, copies_of)
            for copy in copies:
                copy.start()
            for copy in copies:
                copy.wait()
            rows = pl.multiple_of(meta_ref[16] * half_d, half_d)
            output_ref[...] = all_ref[pl.ds(rows, half_d), :]
            shards = count * 8 // 9
            unpack_tiles(tiles_ref, vec_ref, D // shards, FF // shards // 2)

    blocks = own_ref.shape[0] // ROWS
    side = meta_ref[16]
    bias = jnp.concatenate(
        [
            vec_ref[5:6, pl.ds(pl.multiple_of(part * D + side * half_d, LANES), half_d)]
            for part in range(3)
        ],
        1,
    )
    rows = pl.ds(pl.multiple_of(lax.rem(step, blocks) * ROWS, ROWS), ROWS)
    tokens = jnp.where(step < blocks, own_ref[rows, :], peer_ref[rows, :])
    project_rows(tokens, vec_ref, bias, weight_ref[...], tables_ref, packed_ref, one_ref, two_ref)


def project(meta, own, peer, tables, pieces, copies_of):
    rows = 2 * own.shape[0]
    columns = 3 * D // 2
    count = len(pieces)
    scratch = []
    piece_specs = [pl.BlockSpec(memory_space=pltpu.VMEM)] * count
    if copies_of is not None:
        scratch = [
            pltpu.VMEM((D, D), BF16),
            pltpu.VMEM((D, LANES), BF16),
            pltpu.SemaphoreType.DMA((copies_number(copies_of),)),
        ]
        spaces = [pltpu.HBM if 0 < number < 7 else pltpu.VMEM for number in range(count)]
        piece_specs = [pl.BlockSpec(memory_space=space) for space in spaces]
        pieces = [pltpu.with_memory_space_constraint(p, space) for p, space in zip(pieces, spaces)]
    whole = lambda i, m: (0, 0)
    return pl.pallas_call(
        partial(project_kernel, copies_of, count),
        grid_spec=pltpu.PrefetchScalarGridSpec(
            num_scalar_prefetch=1,
            grid=(rows // ROWS,),
            in_specs=[
                pl.BlockSpec((rows // 2, D), whole),
                pl.BlockSpec((rows // 2, D), whole),
                pl.BlockSpec((3, ROWS, LANES), lambda i, m: (0, i, 0)),
            ]
            + piece_specs,
            out_specs=[
                pl.BlockSpec((ROWS, columns), lambda i, m: (i, 0)),
                pl.BlockSpec((ROWS, D), lambda i, m: (i, 0)),
                pl.BlockSpec((ROWS, D), lambda i, m: (i, 0)),
                pl.BlockSpec((D, columns), whole),
                pl.BlockSpec((D // 2, D), whole),
                pl.BlockSpec((8, 3 * D), whole),
            ],
            scratch_shapes=scratch,
        ),
        out_shape=[
            jax.ShapeDtypeStruct((rows, columns), BF16),
            jax.ShapeDtypeStruct((rows, D), BF16),
            jax.ShapeDtypeStruct((rows, D), BF16),
            jax.ShapeDtypeStruct((D, columns), BF16),
            jax.ShapeDtypeStruct((D // 2, D), BF16),
            jax.ShapeDtypeStruct((8, 3 * D), F32),
        ],
        compiler_params=PARAMS,
        name="project",
    )(meta, own, peer, tables, *pieces)


def rotary_lanes(positions):
    lane = jnp.arange(LANES, dtype=jnp.int32) % HD
    half = ROT // 2
    frequency = 10000.0 ** (-(2.0 * f32(lane % half)) / ROT)
    angles = f32(positions)[:, None] * frequency[None, :]
    cosine, sine = jnp.cos(angles), jnp.sin(angles)
    low = (lane < half)[None, :]
    high = ((lane >= half) & (lane < ROT))[None, :]
    return jnp.stack(
        [
            jnp.where(low | high, cosine, 1.0),
            jnp.where(low, -sine, 0.0),
            jnp.where(high, sine, 0.0),
        ]
    )


CONTRACT_ROWS = (((0,), (0,)), ((), ()))
CONTRACT_LAST = (((1,), (1,)), ((), ()))


def dot_rows(left, right):
    return lax.dot_general(left, right, CONTRACT_ROWS, preferred_element_type=F32)


def dot_last(left, right):
    return lax.dot_general(left, right, CONTRACT_LAST, preferred_element_type=F32)


def spread(meta_ref, total_ref, keep_ref, sent_ref, stride=None, offset=0):
    count, rows = keep_ref.shape[0], keep_ref.shape[1]
    stride = stride or rows
    for distance in range(count):
        if sent_ref is None:
            first = distance * stride + offset
            keep_ref[distance] = total_ref[first : first + rows, :]
        else:
            near = pl.multiple_of(meta_ref[distance] * stride + offset, rows)
            keep_ref[distance] = total_ref[pl.ds(near, rows), :]
            far = pl.multiple_of(meta_ref[8 + distance] * stride + offset, rows)
            sent_ref[distance] = bf16(total_ref[pl.ds(far, rows), :])


def grads_out(columns, block, depth, shards, ring, place=None):
    count = 8 if ring else shards
    place = place or (lambda i: i)
    specs = [pl.BlockSpec((count, depth, block), lambda i, m: (0, 0, place(i)))]
    shapes = [jax.ShapeDtypeStruct((count, depth, columns), F32)]
    if ring:
        specs.append(pl.BlockSpec((count, depth, block), lambda i, m: (0, 0, place(i))))
        shapes.append(jax.ShapeDtypeStruct((count, depth, columns), BF16))
    return specs, shapes


def first_grads_kernel(
    ring, meta_ref, one_ref, grads_ref, context_ref, act_own, act_peer, own_ref, peer_ref, *refs
):
    keep_ref, sent_ref = refs[0], refs[1] if ring else None
    total_ref, tall_ref = refs[-2:]
    step = pl.program_id(0)
    half_d = D // 2
    half = own_ref.shape[0]
    depth = keep_ref.shape[1]

    @pl.when(step < 3)
    def _():
        total_ref[...] = dot_rows(one_ref[...], grads_ref[0])

    @pl.when((step == 3) | (step == 4))
    def _():
        side = meta_ref[16]
        here = pl.ds(pl.multiple_of(side * half_d, half_d), half_d)
        there = pl.ds(pl.multiple_of((1 - side) * half_d, half_d), half_d)
        total_ref[there, :] = jnp.zeros((half_d, total_ref.shape[1]), F32)
        total_ref[here, :] = dot_rows(context_ref[:half], own_ref[...]) + dot_rows(
            context_ref[half:], peer_ref[...]
        )

    @pl.when(step < 5)
    def _():
        spread(meta_ref, total_ref, keep_ref, sent_ref)

    @pl.when((step == 5) | (step == 7))
    def _():
        tall_ref[...] = dot_rows(act_own[...], own_ref[...]) + dot_rows(
            act_peer[...], peer_ref[...]
        )
        spread(meta_ref, tall_ref, keep_ref, sent_ref, 2 * depth, 0)

    @pl.when((step == 6) | (step == 8))
    def _():
        spread(meta_ref, tall_ref, keep_ref, sent_ref, 2 * depth, depth)


def first_grads(meta, one, grads, context, act_own, act_peer, own, peer, depth, shards, ring):
    rows = one.shape[0]
    half_d = D // 2
    half_ff = FF // 2

    def place(i):
        return jnp.where(i == 6, 7, jnp.where(i == 7, 6, i))

    specs, shapes = grads_out(9 * half_d, half_d, depth, shards, ring, place)
    whole = lambda i, m: (0, 0)
    late = lambda i, m: (0, jnp.where((i == 4) | (i > 6), 1, 0))
    return pl.pallas_call(
        partial(first_grads_kernel, ring),
        grid_spec=pltpu.PrefetchScalarGridSpec(
            num_scalar_prefetch=1,
            grid=(9,),
            in_specs=[
                pl.BlockSpec((rows, D), whole),
                pl.BlockSpec((1, rows, half_d), lambda i, m: (jnp.minimum(i, 2), 0, 0)),
                pl.BlockSpec((rows, half_d), whole),
                pl.BlockSpec((rows // 2, half_ff), whole),
                pl.BlockSpec((rows // 2, half_ff), whole),
                pl.BlockSpec((rows // 2, half_d), late),
                pl.BlockSpec((rows // 2, half_d), late),
            ],
            out_specs=specs,
            scratch_shapes=[
                pltpu.VMEM((D, half_d), F32),
                pltpu.VMEM((half_ff, half_d), F32),
            ],
        ),
        out_shape=shapes,
        compiler_params=PARAMS,
        name="first_grads",
    )(meta, one, grads, context, act_own, act_peer, own, peer)


def joint_back_kernel(
    tokens_own_ref, tokens_peer_ref, up_ref, grads_ref, weight_ref, vec_ref, scaled_ref, sums_ref
):
    step = pl.program_id(0)
    half_d = D // 2
    blocks = tokens_own_ref.shape[0] // ROWS
    rows = pl.ds(pl.multiple_of(lax.rem(step, blocks) * ROWS, ROWS), ROWS)
    tokens = jnp.where(step < blocks, tokens_own_ref[rows, :], tokens_peer_ref[rows, :])
    unit, _ = unit_of(f32(tokens))
    total = dot_last(grads_ref[0], weight_ref[:, :half_d])
    for part in (1, 2):
        total = total + dot_last(
            grads_ref[part], weight_ref[:, part * half_d : (part + 1) * half_d]
        )
    scaled_ref[...] = total * vec_ref[0:1, :D]

    @pl.when(step == 0)
    def _():
        sums_ref[...] = jnp.zeros_like(sums_ref)

    sums_ref[0:1, :] += jnp.sum(total * unit, axis=0, keepdims=True)
    sums_ref[1:2, :] += jnp.sum(total, axis=0, keepdims=True)
    for part in range(3):
        sums_ref[2 + part : 3 + part, :half_d] += jnp.sum(
            f32(grads_ref[part]), axis=0, keepdims=True
        )

    @pl.when(step < blocks)
    def _():
        sums_ref[5:6, :] += jnp.sum(f32(up_ref[rows, :]), axis=0, keepdims=True)


def joint_back(own, peer, up, grads, weight, vecs):
    rows = grads.shape[1]
    half_d = D // 2
    whole = lambda i: (0, 0)
    return pl.pallas_call(
        joint_back_kernel,
        grid=(rows // ROWS,),
        in_specs=[
            pl.BlockSpec((rows // 2, D), whole),
            pl.BlockSpec((rows // 2, D), whole),
            pl.BlockSpec((rows // 2, D), whole),
            pl.BlockSpec((3, ROWS, half_d), lambda i: (0, i, 0)),
            pl.BlockSpec((D, 3 * half_d), whole),
            pl.BlockSpec((8, 3 * D), whole),
        ],
        out_specs=[
            pl.BlockSpec((ROWS, D), lambda i: (i, 0)),
            pl.BlockSpec((8, D), whole),
        ],
        out_shape=[
            jax.ShapeDtypeStruct((rows, D), F32),
            jax.ShapeDtypeStruct((8, D), F32),
        ],
        compiler_params=PARAMS,
        name="joint_back",
    )(own, peer, up, grads, weight, vecs)


def gelu_parts(v):
    phi = 0.5 * (1.0 + lax.erf(v * np.float32(np.sqrt(0.5))))
    density = jnp.exp(-0.5 * v * v) * np.float32(1.0 / np.sqrt(2.0 * np.pi))
    return v * phi, phi + v * density


def forward_kernel(copies_of, count, meta_ref, two_ref, context_ref, output_ref, vec_ref, *refs):
    pieces, rest = refs[:count], refs[count:]
    act_ref, slope_ref, out_ref = rest[:3]
    if copies_of is None:
        expand_ref, contract_ref = pieces
    else:
        expand_ref, contract_ref, sem = rest[3:6]

        @pl.when(pl.program_id(0) == 0)
        def _():
            copies = piece_copies(meta_ref, pieces, (expand_ref, contract_ref), sem, copies_of)
            for copy in copies:
                copy.start()
            for copy in copies:
                copy.wait()

    shift = jnp.where(meta_ref[16] == 0, vec_ref[6:7, : FF // 2], vec_ref[7:8, : FF // 2])
    expanded = jnp.dot(two_ref[...], expand_ref[...], preferred_element_type=F32) + shift
    activated, slope = gelu_parts(expanded)
    slope_ref[...] = slope
    activated = bf16(activated)
    act_ref[...] = activated
    attended = jnp.dot(context_ref[...], output_ref[...], preferred_element_type=F32)
    mixed = jnp.dot(activated, contract_ref[...], preferred_element_type=F32)
    out_ref[...] = (attended + mixed).astype(out_ref.dtype)


def forward(meta, two, context, output, vecs, pieces, copies_of, first, rows, out_type):
    half_ff = FF // 2
    count = len(pieces)
    whole = lambda i, m: (0, 0)
    scratch = []
    out_specs = [
        pl.BlockSpec((ROWS, half_ff), lambda i, m: (i, 0)),
        pl.BlockSpec((ROWS, half_ff), lambda i, m: (i, 0)),
        pl.BlockSpec((ROWS, D), lambda i, m: (i, 0)),
    ]
    out_shape = [
        jax.ShapeDtypeStruct((rows, half_ff), BF16),
        jax.ShapeDtypeStruct((rows, half_ff), F32),
        jax.ShapeDtypeStruct((rows, D), out_type),
    ]
    piece_specs = [
        pl.BlockSpec((D, half_ff), whole),
        pl.BlockSpec((half_ff, D), whole),
    ]
    if copies_of is not None:
        scratch = [pltpu.SemaphoreType.DMA((copies_number(copies_of),))]
        out_specs += piece_specs
        out_shape += [
            jax.ShapeDtypeStruct((D, half_ff), BF16),
            jax.ShapeDtypeStruct((half_ff, D), BF16),
        ]
        piece_specs = [pl.BlockSpec(memory_space=pltpu.VMEM)] * count
        pieces = in_memory(pltpu.VMEM, pieces)
    base = first // ROWS
    return pl.pallas_call(
        partial(forward_kernel, copies_of, count),
        grid_spec=pltpu.PrefetchScalarGridSpec(
            num_scalar_prefetch=1,
            grid=(rows // ROWS,),
            in_specs=[
                pl.BlockSpec((ROWS, D), lambda i, m: (base + i, 0)),
                pl.BlockSpec((ROWS, D // 2), lambda i, m: (base + i, 0)),
                pl.BlockSpec((D // 2, D), whole),
                pl.BlockSpec((8, 3 * D), whole),
            ]
            + piece_specs,
            out_specs=out_specs,
            scratch_shapes=scratch,
        ),
        out_shape=out_shape,
        compiler_params=PARAMS,
        name="forward_peer" if first else "forward_own",
    )(meta, two, context, output, vecs, *pieces)


def backward_kernel(
    own, tokens_ref, up_ref, slope_ref, scaled_ref, expand_ref, contract_ref, vec_ref,
    grad_ref, pulled_ref, sums_ref
):
    slope_grad = dot_last(up_ref[...], contract_ref[...])
    grad = bf16(slope_grad * slope_ref[...])
    grad_ref[...] = grad
    total = dot_last(grad, expand_ref[...])
    unit, scale = unit_of(f32(tokens_ref[...]))
    scaled = scaled_ref[...] + total * vec_ref[2:3, :D]
    pulled = (
        scaled
        - jnp.mean(scaled, axis=-1, keepdims=True)
        - unit * jnp.mean(scaled * unit, axis=-1, keepdims=True)
    ) * scale
    if own:
        pulled = pulled + f32(up_ref[...])
    pulled_ref[...] = pulled.astype(pulled_ref.dtype)

    @pl.when(pl.program_id(0) == 0)
    def _():
        sums_ref[...] = jnp.zeros_like(sums_ref)

    sums_ref[0:1, :D] += jnp.sum(total * unit, axis=0, keepdims=True)
    sums_ref[1:2, :D] += jnp.sum(total, axis=0, keepdims=True)
    sums_ref[2:3, :] += jnp.sum(f32(grad), axis=0, keepdims=True)


def backward(tokens, up, slope, scaled, expand, contract, vecs, own):
    rows = tokens.shape[0]
    half_ff = FF // 2
    base = 0 if own else rows // ROWS
    whole = lambda i: (0, 0)
    block = lambda i: (i, 0)
    return pl.pallas_call(
        partial(backward_kernel, own),
        grid=(rows // ROWS,),
        in_specs=[
            pl.BlockSpec((ROWS, D), block),
            pl.BlockSpec((ROWS, D), block),
            pl.BlockSpec((ROWS, half_ff), block),
            pl.BlockSpec((ROWS, D), lambda i: (base + i, 0)),
            pl.BlockSpec((D, half_ff), whole),
            pl.BlockSpec((half_ff, D), whole),
            pl.BlockSpec((8, 3 * D), whole),
        ],
        out_specs=[
            pl.BlockSpec((ROWS, half_ff), block),
            pl.BlockSpec((ROWS, D), block),
            pl.BlockSpec((8, half_ff), whole),
        ],
        out_shape=[
            jax.ShapeDtypeStruct((rows, half_ff), BF16),
            jax.ShapeDtypeStruct((rows, D), F32 if own else BF16),
            jax.ShapeDtypeStruct((8, half_ff), F32),
        ],
        compiler_params=PARAMS,
        name="backward_own" if own else "backward_peer",
    )(tokens, up, slope, scaled, expand, contract, vecs)


def weight_grads_kernel(ring, sums, meta_ref, left_own, left_peer, right_own, right_peer, *refs):
    parts, refs = refs[:sums], refs[sums:]
    keep_ref, sent_ref, total_ref = refs[0], refs[1] if ring else None, refs[2 if ring else 1]
    step = pl.program_id(0)

    def products():
        total_ref[...] = dot_rows(left_own[...], right_own[...]) + dot_rows(
            left_peer[...], right_peer[...]
        )

    if sums:
        vec_ref = refs[3]
        last = pl.num_programs(0) - 1
        pl.when(step < last)(products)

        @pl.when(step == last)
        def _():
            collect(meta_ref[16], *parts, vec_ref)
            depth = keep_ref.shape[1]
            width = vec_ref.shape[1]
            total_ref[...] = jnp.zeros_like(total_ref)
            values = vec_ref[...]
            for device in range(D // depth):

                def rolled(size):
                    shift = device * size
                    return pltpu.roll(values, width - shift, 1) if shift else values

                row = device * depth
                total_ref[row : row + 8, :LANES] = rolled(depth)[:, :LANES]
                bias = rolled(3 * depth)
                total_ref[row + 8 : row + 9, :LANES] = bias[5:6, :LANES]
                total_ref[row + 9 : row + 10, :LANES] = bias[5:6, LANES : 2 * LANES]
                total_ref[row + 16 : row + 18, :LANES] = rolled(2 * depth)[6:8, :LANES]

    else:
        products()
    spread(meta_ref, total_ref, keep_ref, sent_ref)


def weight_grads(meta, left, right, rows_each, shards, ring, sums=()):
    (left_own, left_peer, left_shift), (right_own, right_peer) = left, right
    rows = right_own.shape[0]
    depth = left_own.shape[1]
    block = 384
    steps = right_own.shape[1] // block
    columns = right_own.shape[1] + (LANES if sums else 0)
    specs, shapes = grads_out(columns, block, rows_each, shards, ring)
    column = lambda i, m: (0, jnp.minimum(i, steps - 1))
    scratch = [pltpu.VMEM((depth, block), F32)]
    if sums:
        scratch.append(pltpu.VMEM((8, 3 * D), F32))
    return pl.pallas_call(
        partial(weight_grads_kernel, ring, len(sums)),
        grid_spec=pltpu.PrefetchScalarGridSpec(
            num_scalar_prefetch=1,
            grid=(pl.cdiv(columns, block),),
            in_specs=[
                pl.BlockSpec((rows, depth), lambda i, m: (0, 0)),
                pl.BlockSpec((rows, depth), lambda i, m: (left_shift, 0)),
                pl.BlockSpec((rows, block), column),
                pl.BlockSpec((rows, block), column),
            ]
            + [pl.BlockSpec(part.shape, lambda i, m: (0, 0)) for part in sums],
            out_specs=specs,
            scratch_shapes=scratch,
        ),
        out_shape=shapes,
        compiler_params=PARAMS,
    )(meta, left_own, left_peer, right_own, right_peer, *sums)


def attention_kernel(
    side_ref, q_ref, k_ref, v_ref, own_ref, peer_ref, output_ref, tables_ref, *refs
):
    context_ref, grads_ref, dk_acc, dv_acc = refs[-4:]
    rows = q_ref.shape[0]
    half = rows // 2
    block = min(256, half)
    start_one = pl.multiple_of(side_ref[16] * half, half)
    start_two = pl.multiple_of((1 - side_ref[16]) * half, half)

    def natural(ref):
        return jnp.concatenate([ref[pl.ds(start_one, half), :], ref[pl.ds(start_two, half), :]], 0)

    q = natural(q_ref) * jnp.asarray(0.125, BF16)
    k = natural(k_ref)
    v = natural(v_ref)
    up_own = bf16(dot_last(own_ref[...], output_ref[...]))
    up_peer = bf16(dot_last(peer_ref[...], output_ref[...]))
    second = side_ref[16] == 1
    up = jnp.concatenate(
        [jnp.where(second, up_peer, up_own), jnp.where(second, up_own, up_peer)], 0
    )
    lane = lax.broadcasted_iota(jnp.int32, (1, LANES), 1)
    contract_last = (((1,), (1,)), ((), ()))
    contract_first = (((0,), (0,)), ((), ()))
    dk_acc[...] = jnp.zeros_like(dk_acc)
    dv_acc[...] = jnp.zeros_like(dv_acc)
    below = lax.broadcasted_iota(jnp.int32, (block, block), 0) <= lax.broadcasted_iota(
        jnp.int32, (block, block), 1
    )

    def rotate_back(values, start):
        cosine = tables_ref[0, pl.ds(start, values.shape[0]), :]
        plus = tables_ref[1, pl.ds(start, values.shape[0]), :]
        minus = tables_ref[2, pl.ds(start, values.shape[0]), :]
        return (
            values * cosine
            - pltpu.roll(values, LANES - 8, 1) * plus
            - pltpu.roll(values, 8, 1) * minus
        )

    def local(row):
        return pl.multiple_of(
            (start_one if row < half else start_two) + (row if row < half else row - half), block
        )

    for number in range(rows // block):
        low, high = number * block, (number + 1) * block
        context_total = None
        dq_total = None
        for head in range(LANES // HD):
            mask = (lane // HD == head).astype(BF16)
            q_head = q[low:high] * mask
            up_head = up[low:high] * mask
            k_head = k[:high] * mask
            v_head = v[:high] * mask
            scores = lax.dot_general(k[:high], q_head, contract_last, preferred_element_type=F32)
            diagonal = jnp.where(below, scores[low:high], -1e30)
            scores = diagonal if low == 0 else jnp.concatenate([scores[:low], diagonal], 0)
            highest = jnp.max(scores, axis=0, keepdims=True)
            expo = jnp.exp(scores - highest)
            total = jnp.sum(expo, axis=0, keepdims=True)
            probs = expo * (1.0 / total)
            weights = probs.astype(BF16)
            weights_grad = lax.dot_general(
                v[:high], up_head, contract_last, preferred_element_type=F32
            )
            inner = jnp.sum(probs * weights_grad, axis=0, keepdims=True)
            scores_grad = (probs * (weights_grad - inner)).astype(BF16)
            context = lax.dot_general(
                v_head, weights, contract_first, preferred_element_type=F32
            )
            dq = lax.dot_general(k_head, scores_grad, contract_first, preferred_element_type=F32)
            context_total = context if context_total is None else context_total + context
            dq_total = dq if dq_total is None else dq_total + dq
            dv_acc[:high, :] += jnp.dot(weights, up_head, preferred_element_type=F32)
            dk_acc[:high, :] += jnp.dot(scores_grad, q_head, preferred_element_type=F32)
        place = local(low)
        context_ref[pl.ds(place, block), :] = context_total.T.astype(BF16)
        dq_low = (dq_total.T * 0.125).astype(BF16).astype(F32)
        grads_ref[0, pl.ds(place, block), :] = rotate_back(dq_low, place).astype(BF16)
    for number in range(rows // block):
        low = number * block
        place = local(low)
        dk_low = dk_acc[low : low + block, :].astype(BF16).astype(F32)
        grads_ref[1, pl.ds(place, block), :] = rotate_back(dk_low, place).astype(BF16)
        grads_ref[2, pl.ds(place, block), :] = dv_acc[low : low + block, :].astype(BF16)


def attention(side, packed, own, peer, output, tables, number, before):
    rows, columns = packed.shape[0], packed.shape[1] // 3
    pairs = columns // LANES
    ins = [side, packed, packed, packed, own, peer, output, tables]
    return pl.pallas_call(
        attention_kernel,
        grid_spec=pltpu.PrefetchScalarGridSpec(
            num_scalar_prefetch=1,
            grid=(1,),
            in_specs=[
                pl.BlockSpec((rows, LANES), lambda i, s: (0, number)),
                pl.BlockSpec((rows, LANES), lambda i, s: (0, pairs + number)),
                pl.BlockSpec((rows, LANES), lambda i, s: (0, 2 * pairs + number)),
                pl.BlockSpec((rows // 2, D), lambda i, s: (0, 0)),
                pl.BlockSpec((rows // 2, D), lambda i, s: (0, 0)),
                pl.BlockSpec((LANES, D), lambda i, s: (number, 0)),
                pl.BlockSpec((3, rows, LANES), lambda i, s: (0, 0, 0)),
            ]
            + [pl.BlockSpec(memory_space=pl.ANY)] * len(before),
            out_specs=[
                pl.BlockSpec((rows, LANES), lambda i, s: (0, number)),
                pl.BlockSpec((3, rows, LANES), lambda i, s: (0, 0, number)),
            ],
            scratch_shapes=[pltpu.VMEM((rows, LANES), F32), pltpu.VMEM((rows, LANES), F32)],
        ),
        out_shape=[
            jax.ShapeDtypeStruct((rows, columns), BF16),
            jax.ShapeDtypeStruct((3, rows, columns), BF16),
        ],
        input_output_aliases={len(ins) + i: i for i in range(len(before))},
        compiler_params=PARAMS,
    )(*ins, *before)


def finish_first_kernel(side_ref, mine_ref, peer_ref, joint_ref, output_ref, contract_ref):
    side = side_ref[0]
    half_d = D // 2
    depth = mine_ref.shape[0]
    for source, plane in ((mine_ref, side), (peer_ref, 1 - side)):
        for part in range(3):
            start = pl.multiple_of(part * D + plane * half_d, LANES)
            joint_ref[:, pl.ds(start, half_d)] = f32(
                source[:, part * half_d : (part + 1) * half_d]
            )
        for part in range(2):
            start = pl.multiple_of((plane * 2 + part) * depth, depth)
            columns = slice(5 * half_d + part * D, 5 * half_d + (part + 1) * D)
            contract_ref[pl.ds(start, depth), :] = f32(source[:, columns])
    columns = slice(3 * half_d, 5 * half_d)
    output_ref[...] = mine_ref[:, columns] + f32(peer_ref[:, columns])


def finish_first(side, mine, peer):
    depth = mine.shape[0]
    whole = lambda i, s: (0, 0)
    shapes = [(depth, 3 * D), (depth, D), (4 * depth, D)]
    return pl.pallas_call(
        finish_first_kernel,
        grid_spec=pltpu.PrefetchScalarGridSpec(
            num_scalar_prefetch=1,
            grid=(1,),
            in_specs=[pl.BlockSpec(mine.shape, whole), pl.BlockSpec(peer.shape, whole)],
            out_specs=[pl.BlockSpec(shape, whole) for shape in shapes],
        ),
        out_shape=[jax.ShapeDtypeStruct(shape, F32) for shape in shapes],
        compiler_params=PARAMS,
        name="finish_first",
    )(side, mine, peer)


def finish_expand_kernel(shards, side_ref, mine_ref, peer_ref, expand_ref, *outs):
    half_ff = FF // 2
    wide = half_ff // shards
    depth = mine_ref.shape[0]
    here = side_ref[0] == 0
    mine, peer = mine_ref[:, :half_ff], f32(peer_ref[:, :half_ff])
    zero, one = jnp.where(here, mine, peer), jnp.where(here, peer, mine)
    for device in range(shards):
        columns = slice(device * wide, (device + 1) * wide)
        expand_ref[:, 2 * device * wide : (2 * device + 1) * wide] = zero[:, columns]
        expand_ref[:, (2 * device + 1) * wide : (2 * device + 2) * wide] = one[:, columns]
    tile = mine_ref[:, half_ff:] + f32(peer_ref[:, half_ff:])
    for row in range(5):
        outs[row][...] = tile[row : row + 1, :depth]
    outs[5][:, :LANES] = tile[8:9, :]
    outs[5][:, LANES:] = tile[9:10, : 3 * depth - LANES]
    outs[6][:, :wide] = tile[16:17, :wide]
    outs[6][:, wide:] = tile[17:18, :wide]


def finish_expand(side, mine, peer, shards):
    depth = mine.shape[0]
    whole = lambda i, s: (0, 0)
    shapes = [(depth, FF)] + [(1, depth)] * 5 + [(1, 3 * depth), (1, FF // shards)]
    outs = pl.pallas_call(
        partial(finish_expand_kernel, shards),
        grid_spec=pltpu.PrefetchScalarGridSpec(
            num_scalar_prefetch=1,
            grid=(1,),
            in_specs=[pl.BlockSpec(mine.shape, whole), pl.BlockSpec(peer.shape, whole)],
            out_specs=[pl.BlockSpec(shape, whole) for shape in shapes],
        ),
        out_shape=[jax.ShapeDtypeStruct(shape, F32) for shape in shapes],
        compiler_params=PARAMS,
        name="finish_expand",
    )(side, mine, peer)
    return outs[0], [out.reshape(-1) for out in outs[1:]]


def finish_out_kernel(tokens_ref, mine_ref, peer_ref, vec_ref, out_ref):
    out_ref[...] = bf16(
        f32(tokens_ref[...]) + mine_ref[...] + f32(peer_ref[...]) + vec_ref[4:5, :D]
    )


def finish_tokens_kernel(mine_ref, peer_ref, out_ref):
    out_ref[...] = mine_ref[...] + f32(peer_ref[...])


def finish_rows(kernel, ins, kept):
    rows = ins[0].shape[0]
    block = lambda i: (i, 0)
    specs = [pl.BlockSpec((ROWS // 2, D), block) for _ in ins[:3]]
    if len(ins) > 3:
        specs.append(pl.BlockSpec(ins[3].shape, lambda i: (0, 0)))
    return pl.pallas_call(
        kernel,
        grid=(rows // (ROWS // 2),),
        in_specs=specs,
        out_specs=pl.BlockSpec((ROWS // 2, D), block),
        out_shape=jax.ShapeDtypeStruct((rows, D), kept),
        compiler_params=PARAMS,
    )(*ins)


def layer(
    tokens,
    first_norm_gain,
    first_norm_shift,
    second_norm_gain,
    second_norm_shift,
    projection_weight,
    projection_bias,
    output_weight,
    output_bias,
    expand_weight,
    expand_bias,
    contract_weight,
    contract_bias,
    cotangent,
):
    shards = lax.axis_size("fsdp")
    ring = shards == RING_SIZE
    me = lax.axis_index("fsdp").astype(jnp.int32)
    side = lax.axis_index("seq").astype(jnp.int32)
    rows = tokens.shape[1]
    depth = D // shards
    wide = FF // shards // 2
    half_d, half_ff = D // 2, FF // 2
    split = 3 * half_d
    here = side == 0

    own_tokens, own_up = tokens[0], cotangent[0]
    peer_tokens = side_swap(own_tokens)
    peer_up = side_swap(own_up)

    vectors = [
        first_norm_gain,
        first_norm_shift,
        second_norm_gain,
        second_norm_shift,
        output_bias,
        contract_bias,
    ]
    by_side = expand_weight.reshape(depth, shards, 2, wide)
    expand_half = jnp.where(here, by_side[:, :, 0], by_side[:, :, 1]).reshape(depth, half_ff)
    contract_half = jnp.where(here, contract_weight[:wide], contract_weight[wide:])
    first_copies = second_copies = None
    if ring:
        order = lax.dynamic_index_in_dim(jnp.asarray(ring_table()), me, 0, keepdims=False)
        meta = jnp.concatenate([order, side.reshape(1)])
        first_shard = pack(
            side.reshape(1),
            projection_weight,
            output_weight,
            jnp.concatenate(vectors + [projection_bias, expand_bias]).reshape(1, -1),
        )
        second_shard = jnp.concatenate(
            [expand_half[:, :D], expand_half[:, D:], contract_half], 0
        )
        middle = 8 * LANES
        first_pieces = ring_gather(first_shard, 1, middle)
        second_pieces = ring_gather(second_shard, 0, 2 * depth)

        def first_copies(part, device):
            lines = device_rows(device, depth)
            every = pl.ds(0, depth)
            if part == "a":
                return [((every, pl.ds(0, middle)), 0, (lines, pl.ds(0, middle)))]
            shift = middle if part == "b" else 0
            return [
                ((every, pl.ds(0, split - shift)), 0, (lines, pl.ds(shift, split - shift))),
                ((every, pl.ds(split - shift, D)), 1, (lines, pl.ds(0, D))),
                ((every, pl.ds(split - shift + D, LANES)), 2, (lines, pl.ds(0, LANES))),
            ]

        def second_copies(part, device):
            lines = device_rows(device, depth)
            low = ((pl.ds(0, depth), pl.ds(0, D)), 0, (lines, pl.ds(0, D)))
            high = ((pl.ds(depth, depth), pl.ds(0, D)), 0, (lines, pl.ds(D, D)))
            start = 0 if part == "b" else 2 * depth
            last = ((pl.ds(start, wide), pl.ds(0, D)), 1, (device_rows(device, wide), pl.ds(0, D)))
            return {"all": [low, high, last], "a": [low, high], "b": [last]}[part]

    else:
        gather = partial(lax.all_gather, axis_name="fsdp", axis=0, tiled=True)
        meta = jnp.concatenate([jnp.zeros((16,), jnp.int32), side.reshape(1)])
        by_half = projection_weight.reshape(depth, 3, 2, half_d)
        projection_half = jnp.where(here, by_half[:, :, 0], by_half[:, :, 1])
        first_full = gather(
            jnp.concatenate([projection_half.reshape(depth, split), output_weight], 1)
        )
        gathered = [f32(gather(v)) for v in vectors]
        shift = gather(expand_bias).reshape(shards, 2, wide)
        vecs = jnp.zeros((8, 3 * D), F32)
        for row, value in enumerate(gathered[:4]):
            vecs = vecs.at[row, :D].set(value)
        vecs = vecs.at[4, :D].set(gathered[4] + gathered[5])
        vecs = vecs.at[5].set(f32(gather(projection_bias)))
        for part in range(2):
            vecs = vecs.at[6 + part, :half_ff].set(f32(shift[:, part].reshape(half_ff)))
        first_pieces = [first_full, vecs]
        second_pieces = [gather(expand_half), gather(contract_half)]

    row_numbers = jnp.arange(rows, dtype=jnp.int32)
    positions = jnp.concatenate([side * rows + row_numbers, (1 - side) * rows + row_numbers])
    tables = rotary_lanes(positions)
    packed, one, two, projection_full, output_half, vecs = project(
        meta, own_tokens, peer_tokens, tables, first_pieces, first_copies
    )
    context, grads = before = attention(
        meta, packed, own_up, peer_up, output_half, tables, 0, ()
    )
    for number in range(1, half_d // LANES):
        context, grads = before = attention(
            meta, packed, own_up, peer_up, output_half, tables, number, before
        )

    peer_parts = forward(
        meta, two, context, output_half, vecs, second_pieces, second_copies, rows, rows, BF16
    )
    act_peer, slope_peer, out_peer = peer_parts[:3]
    expand_full, contract_full = peer_parts[3:] if ring else second_pieces
    out_arrived = side_swap(out_peer)
    act_own, slope_own, out_own = forward(
        meta, two, context, output_half, vecs, [expand_full, contract_full], None, 0, rows, F32
    )
    first_parts = list(
        first_grads(
            meta, one, grads, context, act_own, act_peer, own_up, peer_up, depth, shards, ring
        )
    )
    grads, first_parts[-1] = lax.optimization_barrier((grads, first_parts[-1]))
    if ring:
        first, first_low = ring_scatter(*first_parts, 14 * LANES)
        first_peer = side_swap(first_low)
    else:
        first = lax.psum_scatter(first_parts[0], "fsdp", scatter_dimension=0, tiled=False)
        first_peer = side_swap(bf16(first))

    scaled, sums_one = joint_back(
        own_tokens, peer_tokens, own_up, grads, projection_full, vecs
    )
    grad_peer, pulled_peer, sums_peer = backward(
        peer_tokens, peer_up, slope_peer, scaled, expand_full, contract_full, vecs, False
    )
    slope_own, pulled_peer = lax.optimization_barrier((slope_own, pulled_peer))
    pulled_arrived = side_swap(pulled_peer)
    grad_own, pulled_own, sums_own = backward(
        own_tokens, own_up, slope_own, scaled, expand_full, contract_full, vecs, True
    )
    sums = (sums_one, sums_peer, sums_own)
    expand_parts = weight_grads(
        meta, (two, two, 1), (grad_own, grad_peer), depth, shards, ring, sums if ring else ()
    )
    if ring:
        expand, expand_low = ring_scatter(*expand_parts, 7 * LANES)
        expand_peer = side_swap(expand_low)
    else:
        expand = lax.psum_scatter(expand_parts[0], "fsdp", scatter_dimension=0, tiled=False)
        expand_peer = side_swap(bf16(expand))

    layer_output = finish_rows(
        finish_out_kernel, [own_tokens, out_own, out_arrived, vecs], BF16
    )[None]
    tokens_grad = finish_rows(finish_tokens_kernel, [pulled_own, pulled_arrived], F32)[None]
    if ring:
        joint_grad, output_grad, contract_grad = finish_first(side.reshape(1), first, first_peer)
        expand_grad, picked = finish_expand(side.reshape(1), expand, expand_peer, shards)
    else:
        peer = f32(first_peer)
        zero, other = jnp.where(here, first, peer), jnp.where(here, peer, first)
        joint_grad = jnp.stack(
            [
                zero[:, :split].reshape(depth, 3, half_d),
                other[:, :split].reshape(depth, 3, half_d),
            ],
            2,
        ).reshape(depth, 3 * D)
        output_grad = (first + peer)[:, split : split + D]
        last = split + D
        contract_grad = jnp.concatenate(
            [zero[:, last : last + D], zero[:, last + D :], other[:, last : last + D], other[:, last + D :]],
            0,
        )
        peer = f32(expand_peer)
        zero, other = jnp.where(here, expand, peer), jnp.where(here, peer, expand)
        expand_grad = jnp.stack(
            [zero.reshape(depth, shards, wide), other.reshape(depth, shards, wide)], 2
        ).reshape(depth, FF)
        small = lax.psum(collect_sums(meta, *sums), ("fsdp", "seq"))

        def own_part(row, size):
            return lax.dynamic_slice(small, (row, me * size), (1, size))[0]

        picked = [own_part(row, depth) for row in range(5)]
        picked.append(own_part(5, 3 * depth))
        picked.append(jnp.concatenate([own_part(6, wide), own_part(7, wide)]))
    gain_one, shift_one, gain_two, shift_two, bias, joint_bias, expand_bias_grad = picked
    return (
        layer_output,
        tokens_grad,
        gain_one,
        shift_one,
        gain_two,
        shift_two,
        joint_grad,
        joint_bias,
        output_grad,
        bias,
        expand_grad,
        expand_bias_grad,
        contract_grad,
        bias,
    )


def solution(mesh):
    return jax.shard_map(
        layer,
        mesh=mesh,
        in_specs=(
            P("fsdp", "seq", None),
            P("fsdp"),
            P("fsdp"),
            P("fsdp"),
            P("fsdp"),
            P("fsdp", None),
            P("fsdp"),
            P("fsdp", None),
            P("fsdp"),
            P("fsdp", None),
            P("fsdp"),
            P("fsdp", None),
            P("fsdp"),
            P("fsdp", "seq", None),
        ),
        out_specs=(
            P("fsdp", "seq", None),
            P("fsdp", "seq", None),
            P("fsdp"),
            P("fsdp"),
            P("fsdp"),
            P("fsdp"),
            P("fsdp", None),
            P("fsdp"),
            P("fsdp", None),
            P("fsdp"),
            P("fsdp", None),
            P("fsdp"),
            P("fsdp", None),
            P("fsdp"),
        ),
        check_vma=False,
    )
```

```python
from functools import partial

import jax
import jax.numpy as jnp
import numpy as np
from jax import lax
from jax.experimental import pallas as pl
from jax.experimental.pallas import tpu as pltpu
from jax.sharding import PartitionSpec as P

D = 768
HD = 64
FF = 3072
ROT = 16
EPSILON = 1e-05
LANES = 128
ROWS = 256
PARAMS = pltpu.CompilerParams(vmem_limit_bytes=24 << 20)

F32 = jnp.float32
BF16 = jnp.bfloat16


def in_memory(space, values):
    return [pltpu.with_memory_space_constraint(value, space) for value in values]


def f32(value):
    return value.astype(F32)


def bf16(value):
    return value.astype(BF16)


RING_CHIPS = (0, 2, 4, 6, 7, 5, 3, 1)
RING_SIZE = 16


def ring_pairs(step):
    count = len(RING_CHIPS)
    return [
        (RING_CHIPS[i] * 2 + core, RING_CHIPS[(i + step) % count] * 2 + core)
        for i in range(count)
        for core in range(2)
    ]


CLOCKWISE = ring_pairs(1)
COUNTER = ring_pairs(-1)
CORE_SWAP = [(f, f ^ 1) for f in range(RING_SIZE)]
SIDE_SWAP = [(0, 1), (1, 0)]


def ring_table():
    table = np.zeros((RING_SIZE, 16), np.int32)
    for f in range(RING_SIZE):
        place = RING_CHIPS.index(f // 2)
        for distance in range(8):
            chip = RING_CHIPS[(place + distance) % 8]
            table[f, distance] = chip * 2 + f % 2
            table[f, 8 + distance] = chip * 2 + 1 - f % 2
    return table


def clockwise(value):
    return lax.ppermute(value, "fsdp", CLOCKWISE)


def counter(value):
    return lax.ppermute(value, "fsdp", COUNTER)


def core_swap(value):
    return lax.ppermute(value, "fsdp", CORE_SWAP)


def side_swap(value):
    return lax.ppermute(value, "seq", SIDE_SWAP)


PIECE_DISTANCES = (0, 1, 7, 2, 6, 3, 5, 4, 4)
PIECE_PARTS = ("all",) * 7 + ("a", "b")


def ring_gather(shard, split_axis, half):
    size = shard.shape[split_axis]
    right, left = shard, shard
    own, other = [shard], [core_swap(shard)]
    for step in range(1, 5):
        if step < 4:
            left, right = counter(left), clockwise(right)
            fresh = [left, right]
        else:
            fresh = [
                clockwise(lax.slice_in_dim(right, 0, half, axis=split_axis)),
                counter(lax.slice_in_dim(left, half, size, axis=split_axis)),
            ]
        own += fresh
        other += [core_swap(piece) for piece in fresh]
    return own + other


def place_pieces(meta_ref, pieces, outs, sem, copies_of, far):
    copies = []
    for now in (True, False):
        for number, piece in enumerate(pieces):
            if (number in far) != now:
                continue
            core, place = divmod(number, 9)
            device = meta_ref[core * 8 + PIECE_DISTANCES[place]]
            for source, out, target in copies_of(PIECE_PARTS[place], device):
                if now:
                    copy = pltpu.make_async_copy(
                        piece.at[source], outs[out].at[target], sem.at[len(copies)]
                    )
                    copy.start()
                    copies.append(copy)
                else:
                    outs[out][target] = piece[source]
    for copy in copies:
        copy.wait()


FAR_PIECES = range(1, 7)
FAR_COPIES = 32


def device_rows(device, size):
    return pl.ds(device * size if isinstance(device, int) else pl.multiple_of(device * size, size), size)


def tick_kernel(kind, cut, groups, *refs):
    def own(number):
        pairs = refs[2 * groups * number : 2 * groups * (number + 1)]
        parts = [keep[...] + f32(other[...]) for keep, other in zip(pairs[::2], pairs[1::2])]
        return parts[0] if groups == 1 else jnp.concatenate(parts, 1)

    if kind == "first":
        right_out, left_out = refs[2 * groups :]
        total = own(0)
        right_out[...] = bf16(total[:, :cut])
        left_out[...] = bf16(total[:, cut:])
    elif kind == "last":
        right, left, total_out, low_out = refs[2 * groups :]
        total = own(0) + f32(right[...]) + f32(left[...])
        total_out[...] = total
        low_out[...] = bf16(total)
    else:
        right, left, right_out, left_out = refs[4 * groups :]
        total_right, total_left = own(0), own(1)
        if kind == "second":
            right_out[:, :cut] = bf16(total_right[:, :cut] + f32(right[...]))
            right_out[:, cut:] = bf16(total_right[:, cut:])
            left_out[:, :cut] = bf16(total_left[:, :cut])
            left_out[:, cut:] = bf16(total_left[:, cut:] + f32(left[...]))
        else:
            right_out[...] = bf16(total_right + f32(right[...]))
            left_out[...] = bf16(total_left + f32(left[...]))


def ring_scatter(parts, cut):
    rows = parts[0][0].shape[1]
    columns = sum(keep.shape[2] for keep, _ in parts)
    pairs = []
    for keep, sent in parts:
        pairs.append((keep, core_swap(sent)))

    def tick(kind, distances, moving, widths, types):
        ins, specs = [], []
        for distance in distances:
            for pair_of in pairs:
                for array in pair_of:
                    ins.append(array)
                    specs.append(
                        pl.BlockSpec(
                            (None,) + array.shape[1:], lambda i, d=distance: (d, 0, 0)
                        )
                    )
        for array in moving:
            ins.append(array)
            specs.append(pl.BlockSpec(array.shape, lambda i: (0, 0)))
        return pl.pallas_call(
            partial(tick_kernel, kind, cut, len(pairs)),
            grid=(1,),
            in_specs=specs,
            out_specs=[pl.BlockSpec((rows, width), lambda i: (0, 0)) for width in widths],
            out_shape=[
                jax.ShapeDtypeStruct((rows, width), kept) for width, kept in zip(widths, types)
            ],
            compiler_params=PARAMS,
        )(*ins)

    def turn(right, left):
        return clockwise(right), counter(left)

    both, low = [columns] * 2, [BF16] * 2
    moving = turn(*tick("first", (4,), (), [cut, columns - cut], low))
    moving = turn(*tick("second", (3, 5), moving, both, low))
    moving = turn(*tick("middle", (2, 6), moving, both, low))
    moving = turn(*tick("middle", (1, 7), moving, both, low))
    return tick("last", (0,), moving, both, [F32, BF16])


TILE_ROWS = 24


def pack_kernel(side_ref, weight_ref, output_ref, *refs):
    vectors, out_ref, tile = refs[:8], refs[8], refs[9]
    staged, sem = refs[12:20], refs[20]
    sources, targets = (weight_ref, output_ref) + vectors, refs[10:20]
    copies = [
        pltpu.make_async_copy(source, target, sem.at[number])
        for number, (source, target) in enumerate(zip(sources, targets))
    ]
    for copy in copies:
        copy.start()
    half_d = D // 2
    tile[...] = jnp.zeros_like(tile)
    for copy in copies:
        copy.wait()
    weight_ref, output_ref = targets[:2]
    for part in range(3):
        start = pl.multiple_of(part * D + side_ref[0] * half_d, LANES)
        out_ref[:, part * half_d : (part + 1) * half_d] = weight_ref[:, pl.ds(start, half_d)]
    out_ref[:, 3 * half_d : 3 * half_d + D] = output_ref[...]
    three, four = staged[6], staged[7]
    depth = weight_ref.shape[0]
    wide = four.shape[1] // 2
    for row in range(6):
        tile[row : row + 1, :depth] = f32(staged[row][...])
    shift = f32(three[...])
    tile[8:9, :] = shift[:, :LANES]
    tile[9:10, : 3 * depth - LANES] = shift[:, LANES:]
    tile[16:17, :wide] = f32(four[:, :wide])
    tile[17:18, :wide] = f32(four[:, wide:])
    out_ref[:, 3 * half_d + D :] = bf16(tile[...])


def pack(side, weight, output, vectors, three, four):
    depth = weight.shape[0]
    columns = 3 * D // 2 + D + LANES
    vectors = [v.reshape(1, -1) for v in vectors + [three, four]]
    return pl.pallas_call(
        pack_kernel,
        grid_spec=pltpu.PrefetchScalarGridSpec(
            num_scalar_prefetch=1,
            grid=(1,),
            in_specs=[pl.BlockSpec(memory_space=pltpu.HBM)] * 10,
            out_specs=pl.BlockSpec((depth, columns), lambda i, s: (0, 0)),
            scratch_shapes=[pltpu.VMEM((depth, LANES), F32)]
            + [pltpu.VMEM(v.shape, BF16) for v in [weight, output] + vectors]
            + [pltpu.SemaphoreType.DMA((10,))],
        ),
        out_shape=jax.ShapeDtypeStruct((depth, columns), BF16),
        compiler_params=PARAMS,
        name="pack",
    )(side, *in_memory(pltpu.HBM, [weight, output] + vectors))


def unpack_tiles(tiles_ref, vec_ref, depth, wide):
    vec_ref[...] = jnp.zeros_like(vec_ref)
    for device in range(D // depth):
        tile = f32(tiles_ref[device * depth : device * depth + TILE_ROWS, :])
        columns = slice(device * depth, (device + 1) * depth)
        vec_ref[0:4, columns] = tile[0:4, :depth]
        vec_ref[4:5, columns] = tile[4:5, :depth] + tile[5:6, :depth]
        first = device * 3 * depth
        vec_ref[5:6, first : first + LANES] = tile[8:9, :]
        vec_ref[5:6, first + LANES : first + 3 * depth] = tile[9:10, : 3 * depth - LANES]
        vec_ref[6:8, device * wide : (device + 1) * wide] = tile[16:18, :wide]


def collect(side, first_peer, first_own, second_ref, third_ref, out):
    out[...] = jnp.zeros_like(out)
    first = first_peer[...] + first_own[...]
    out[0:2, :D] = first[0:2]
    out[2:4, :D] = second_ref[0:2, :D] + third_ref[0:2, :D]
    out[4:5, :D] = first[5:6]
    half = D // 2
    for part in range(3):
        start = pl.multiple_of(part * D + side * half, LANES)
        out[5:6, pl.ds(start, half)] = first[2 + part : 3 + part, :half]
    expand = second_ref[2:3, :] + third_ref[2:3, :]
    wide = expand.shape[1]
    here = side == 0
    out[6:7, :wide] = jnp.where(here, expand, 0.0)
    out[7:8, :wide] = jnp.where(here, 0.0, expand)


def collect_kernel(meta_ref, *refs):
    collect(meta_ref[16], *refs)


def collect_sums(meta, *sums):
    whole = pl.BlockSpec(memory_space=pltpu.VMEM)
    return pl.pallas_call(
        collect_kernel,
        grid_spec=pltpu.PrefetchScalarGridSpec(
            num_scalar_prefetch=1, grid=(), in_specs=[whole] * 4, out_specs=whole
        ),
        out_shape=jax.ShapeDtypeStruct((8, 3 * D), F32),
        compiler_params=PARAMS,
        name="collect_sums",
    )(meta, *sums)


def unit_of(values):
    average = jnp.mean(values, axis=-1, keepdims=True)
    centred = values - average
    variance = jnp.mean(centred * centred, axis=-1, keepdims=True)
    scale = lax.rsqrt(variance + EPSILON)
    return centred * scale, scale


def unit_kernel(tokens_ref, unit_ref, scale_ref):
    unit, scale = unit_of(f32(tokens_ref[...]))
    unit_ref[...] = unit
    scale_ref[...] = jnp.broadcast_to(scale, scale_ref.shape)


def units(tokens):
    rows = tokens.shape[0]
    block = lambda i: (i, 0)
    return pl.pallas_call(
        unit_kernel,
        grid=(rows // ROWS,),
        in_specs=[pl.BlockSpec((ROWS, D), block)],
        out_specs=[pl.BlockSpec((ROWS, D), block), pl.BlockSpec((ROWS, LANES), block)],
        out_shape=[
            jax.ShapeDtypeStruct((rows, D), F32),
            jax.ShapeDtypeStruct((rows, LANES), F32),
        ],
        compiler_params=PARAMS,
    )(tokens)


def project_rows(unit, vec_ref, bias, weight, tables_ref, packed_ref, one_ref, two_ref):
    one = bf16(unit * vec_ref[0:1, :D] + vec_ref[1:2, :D])
    one_ref[...] = one
    two_ref[...] = bf16(unit * vec_ref[2:3, :D] + vec_ref[3:4, :D])
    projected = jnp.dot(one, weight, preferred_element_type=F32) + bias
    columns = projected.shape[1]
    cosine, plus, minus = tables_ref[0], tables_ref[1], tables_ref[2]
    for low in range(0, columns, LANES):
        piece = projected[:, low : low + LANES]
        if low < columns * 2 // 3:
            piece = (
                piece * cosine
                + pltpu.roll(piece, LANES - 8, 1) * plus
                + pltpu.roll(piece, 8, 1) * minus
            )
        packed_ref[:, low : low + LANES] = bf16(piece)


def project_kernel(copies_of, count, meta_ref, own_ref, peer_ref, tables_ref, *refs):
    pieces, rest = refs[:count], refs[count:]
    packed_ref, one_ref, two_ref, weight_ref, output_ref, vec_ref = rest[:6]
    step = pl.program_id(0)
    half_d = D // 2
    if copies_of is None:
        @pl.when(step == 0)
        def _():
            weight_ref[...] = pieces[0][:, : 3 * half_d]
            rows = pl.multiple_of(meta_ref[16] * half_d, half_d)
            output_ref[...] = pieces[0][pl.ds(rows, half_d), 3 * half_d :]
            vec_ref[...] = pieces[1][...]
    else:
        all_ref, tiles_ref, sem = rest[6:]

        @pl.when(step == 0)
        def _():
            outs = (weight_ref, all_ref, tiles_ref)
            place_pieces(meta_ref, pieces, outs, sem, copies_of, FAR_PIECES)
            rows = pl.multiple_of(meta_ref[16] * half_d, half_d)
            output_ref[...] = all_ref[pl.ds(rows, half_d), :]
            shards = count * 8 // 9
            unpack_tiles(tiles_ref, vec_ref, D // shards, FF // shards // 2)

    blocks = own_ref.shape[0] // ROWS
    side = meta_ref[16]
    bias = jnp.concatenate(
        [
            vec_ref[5:6, pl.ds(pl.multiple_of(part * D + side * half_d, LANES), half_d)]
            for part in range(3)
        ],
        1,
    )
    rows = pl.ds(pl.multiple_of(lax.rem(step, blocks) * ROWS, ROWS), ROWS)
    unit = jnp.where(step < blocks, own_ref[rows, :], peer_ref[rows, :])
    project_rows(unit, vec_ref, bias, weight_ref[...], tables_ref, packed_ref, one_ref, two_ref)


def project(meta, own, peer, tables, pieces, copies_of):
    rows = 2 * own.shape[0]
    columns = 3 * D // 2
    count = len(pieces)
    scratch = []
    piece_specs = [pl.BlockSpec(memory_space=pltpu.VMEM)] * count
    if copies_of is not None:
        scratch = [
            pltpu.VMEM((D, D), BF16),
            pltpu.VMEM((D, LANES), BF16),
            pltpu.SemaphoreType.DMA((FAR_COPIES,)),
        ]
        spaces = [pltpu.HBM if n in FAR_PIECES else pltpu.VMEM for n in range(count)]
        piece_specs = [pl.BlockSpec(memory_space=space) for space in spaces]
        pieces = [pltpu.with_memory_space_constraint(p, space) for p, space in zip(pieces, spaces)]
    whole = lambda i, m: (0, 0)
    return pl.pallas_call(
        partial(project_kernel, copies_of, count),
        grid_spec=pltpu.PrefetchScalarGridSpec(
            num_scalar_prefetch=1,
            grid=(rows // ROWS,),
            in_specs=[
                pl.BlockSpec((rows // 2, D), whole),
                pl.BlockSpec((rows // 2, D), whole),
                pl.BlockSpec((3, ROWS, LANES), lambda i, m: (0, i, 0)),
            ]
            + piece_specs,
            out_specs=[
                pl.BlockSpec((ROWS, columns), lambda i, m: (i, 0)),
                pl.BlockSpec((ROWS, D), lambda i, m: (i, 0)),
                pl.BlockSpec((ROWS, D), lambda i, m: (i, 0)),
                pl.BlockSpec((D, columns), whole),
                pl.BlockSpec((D // 2, D), whole),
                pl.BlockSpec((8, 3 * D), whole),
            ],
            scratch_shapes=scratch,
        ),
        out_shape=[
            jax.ShapeDtypeStruct((rows, columns), BF16),
            jax.ShapeDtypeStruct((rows, D), BF16),
            jax.ShapeDtypeStruct((rows, D), BF16),
            jax.ShapeDtypeStruct((D, columns), BF16),
            jax.ShapeDtypeStruct((D // 2, D), BF16),
            jax.ShapeDtypeStruct((8, 3 * D), F32),
        ],
        compiler_params=PARAMS,
        name="project",
    )(meta, own, peer, tables, *pieces)


def rotary_lanes(positions):
    lane = jnp.arange(LANES, dtype=jnp.int32) % HD
    half = ROT // 2
    frequency = 10000.0 ** (-(2.0 * f32(lane % half)) / ROT)
    angles = f32(positions)[:, None] * frequency[None, :]
    cosine, sine = jnp.cos(angles), jnp.sin(angles)
    low = (lane < half)[None, :]
    high = ((lane >= half) & (lane < ROT))[None, :]
    return jnp.stack(
        [
            jnp.where(low | high, cosine, 1.0),
            jnp.where(low, -sine, 0.0),
            jnp.where(high, sine, 0.0),
        ]
    )


CONTRACT_ROWS = (((0,), (0,)), ((), ()))
CONTRACT_LAST = (((1,), (1,)), ((), ()))


def dot_rows(left, right):
    return lax.dot_general(left, right, CONTRACT_ROWS, preferred_element_type=F32)


def dot_last(left, right):
    return lax.dot_general(left, right, CONTRACT_LAST, preferred_element_type=F32)


def spread(meta_ref, total_ref, keep_ref, sent_ref, stride=None, offset=0):
    count, rows = keep_ref.shape[0], keep_ref.shape[1]
    stride = stride or rows
    for distance in range(count):
        if sent_ref is None:
            first = distance * stride + offset
            keep_ref[distance] = total_ref[first : first + rows, :]
        else:
            near = pl.multiple_of(meta_ref[distance] * stride + offset, rows)
            keep_ref[distance] = total_ref[pl.ds(near, rows), :]
            far = pl.multiple_of(meta_ref[8 + distance] * stride + offset, rows)
            sent_ref[distance] = bf16(total_ref[pl.ds(far, rows), :])


def grads_out(columns, block, depth, shards, ring, place=None):
    count = 8 if ring else shards
    place = place or (lambda i: i)
    specs = [pl.BlockSpec((count, depth, block), lambda i, m: (0, 0, place(i)))]
    shapes = [jax.ShapeDtypeStruct((count, depth, columns), F32)]
    if ring:
        specs.append(pl.BlockSpec((count, depth, block), lambda i, m: (0, 0, place(i))))
        shapes.append(jax.ShapeDtypeStruct((count, depth, columns), BF16))
    return specs, shapes


def joint_grads_kernel(ring, meta_ref, one_ref, grads_ref, context_ref, own_ref, peer_ref, *refs):
    keep_ref, sent_ref, total_ref = refs[0], refs[1] if ring else None, refs[-1]
    step = pl.program_id(0)
    half_d = D // 2
    half = own_ref.shape[0]

    @pl.when(step < 3)
    def _():
        total_ref[...] = dot_rows(one_ref[...], grads_ref[0])

    @pl.when(step >= 3)
    def _():
        side = meta_ref[16]
        here = pl.ds(pl.multiple_of(side * half_d, half_d), half_d)
        there = pl.ds(pl.multiple_of((1 - side) * half_d, half_d), half_d)
        total_ref[there, :] = jnp.zeros((half_d, total_ref.shape[1]), F32)
        total_ref[here, :] = dot_rows(context_ref[:half], own_ref[...]) + dot_rows(
            context_ref[half:], peer_ref[...]
        )

    spread(meta_ref, total_ref, keep_ref, sent_ref)


def joint_grads(meta, one, grads, context, own, peer, depth, shards, ring):
    rows = one.shape[0]
    half_d = D // 2
    specs, shapes = grads_out(5 * half_d, half_d, depth, shards, ring)
    whole = lambda i, m: (0, 0)
    late = lambda i, m: (0, jnp.maximum(i - 3, 0))
    return pl.pallas_call(
        partial(joint_grads_kernel, ring),
        grid_spec=pltpu.PrefetchScalarGridSpec(
            num_scalar_prefetch=1,
            grid=(5,),
            in_specs=[
                pl.BlockSpec((rows, D), whole),
                pl.BlockSpec((1, rows, half_d), lambda i, m: (jnp.minimum(i, 2), 0, 0)),
                pl.BlockSpec((rows, half_d), whole),
                pl.BlockSpec((rows // 2, half_d), late),
                pl.BlockSpec((rows // 2, half_d), late),
            ],
            out_specs=specs,
            scratch_shapes=[pltpu.VMEM((D, half_d), F32)],
        ),
        out_shape=shapes,
        compiler_params=PARAMS,
        name="joint_grads",
    )(meta, one, grads, context, own, peer)


def contract_grads_kernel(ring, meta_ref, act_own, act_peer, own_ref, peer_ref, *refs):
    keep_ref, sent_ref, total_ref = refs[0], refs[1] if ring else None, refs[-1]
    step = pl.program_id(0)
    depth = keep_ref.shape[1]

    @pl.when(lax.rem(step, 2) == 0)
    def _():
        total_ref[...] = dot_rows(act_own[...], own_ref[...]) + dot_rows(
            act_peer[...], peer_ref[...]
        )
        spread(meta_ref, total_ref, keep_ref, sent_ref, 2 * depth, 0)

    @pl.when(lax.rem(step, 2) == 1)
    def _():
        spread(meta_ref, total_ref, keep_ref, sent_ref, 2 * depth, depth)


def contract_grads(meta, act, own, peer, depth, shards, ring):
    rows, half_ff = own.shape[0], act.shape[1]
    block = D // 2
    place = lambda i: lax.rem(i, 2) * 2 + lax.div(i, 2)
    specs, shapes = grads_out(2 * D, block, depth, shards, ring, place)
    whole = lambda i, m: (0, 0)
    column = lambda i, m: (0, lax.div(i, 2))
    return pl.pallas_call(
        partial(contract_grads_kernel, ring),
        grid_spec=pltpu.PrefetchScalarGridSpec(
            num_scalar_prefetch=1,
            grid=(4,),
            in_specs=[
                pl.BlockSpec((rows, half_ff), whole),
                pl.BlockSpec((rows, half_ff), lambda i, m: (1, 0)),
                pl.BlockSpec((rows, block), column),
                pl.BlockSpec((rows, block), column),
            ],
            out_specs=specs,
            scratch_shapes=[pltpu.VMEM((half_ff, block), F32)],
        ),
        out_shape=shapes,
        compiler_params=PARAMS,
        name="contract_grads",
    )(meta, act, act, own, peer)


def joint_back_kernel(own, unit_ref, up_ref, grads_ref, weight_ref, vec_ref, scaled_ref, sums_ref):
    half_d = D // 2
    unit = unit_ref[...]
    total = dot_last(grads_ref[0], weight_ref[:, :half_d])
    for part in (1, 2):
        total = total + dot_last(
            grads_ref[part], weight_ref[:, part * half_d : (part + 1) * half_d]
        )
    scaled_ref[...] = total * vec_ref[0:1, :D]

    @pl.when(pl.program_id(0) == 0)
    def _():
        sums_ref[...] = jnp.zeros_like(sums_ref)

    sums_ref[0:1, :] += jnp.sum(total * unit, axis=0, keepdims=True)
    sums_ref[1:2, :] += jnp.sum(total, axis=0, keepdims=True)
    for part in range(3):
        sums_ref[2 + part : 3 + part, :half_d] += jnp.sum(
            f32(grads_ref[part]), axis=0, keepdims=True
        )
    if own:
        sums_ref[5:6, :] += jnp.sum(f32(up_ref[...]), axis=0, keepdims=True)


def joint_back(unit, up, grads, weight, vecs, own):
    rows = unit.shape[0]
    half_d = D // 2
    base = 0 if own else rows // ROWS
    whole = lambda i: (0, 0)
    block = lambda i: (i, 0)
    return pl.pallas_call(
        partial(joint_back_kernel, own),
        grid=(rows // ROWS,),
        in_specs=[
            pl.BlockSpec((ROWS, D), block),
            pl.BlockSpec((ROWS, D), block),
            pl.BlockSpec((3, ROWS, half_d), lambda i: (0, base + i, 0)),
            pl.BlockSpec((D, 3 * half_d), whole),
            pl.BlockSpec((8, 3 * D), whole),
        ],
        out_specs=[pl.BlockSpec((ROWS, D), block), pl.BlockSpec((8, D), whole)],
        out_shape=[
            jax.ShapeDtypeStruct((rows, D), F32),
            jax.ShapeDtypeStruct((8, D), F32),
        ],
        compiler_params=PARAMS,
        name="joint_back_own" if own else "joint_back_peer",
    )(unit, up, grads, weight, vecs)


def gelu_parts(v):
    phi = 0.5 * (1.0 + lax.erf(v * np.float32(np.sqrt(0.5))))
    density = jnp.exp(-0.5 * v * v) * np.float32(1.0 / np.sqrt(2.0 * np.pi))
    return v * phi, phi + v * density


def forward_kernel(ring, count, meta_ref, two_ref, context_ref, output_ref, vec_ref, *refs):
    pieces, rest = refs[:count], refs[count:]
    act_ref, slope_ref, peer_ref, own_ref = rest[:4]
    step = pl.program_id(0)
    if ring:
        expand_ref, contract_ref, copies_of = rest[4], rest[5], ring

        @pl.when(step == 0)
        def _():
            place_pieces(meta_ref, pieces, (expand_ref, contract_ref), None, copies_of, ())
    else:
        expand_ref, contract_ref = pieces

    shift = jnp.where(meta_ref[16] == 0, vec_ref[6:7, : FF // 2], vec_ref[7:8, : FF // 2])
    expanded = jnp.dot(two_ref[...], expand_ref[...], preferred_element_type=F32) + shift
    activated, slope = gelu_parts(expanded)
    slope_ref[...] = slope
    activated = bf16(activated)
    act_ref[...] = activated
    attended = jnp.dot(context_ref[...], output_ref[...], preferred_element_type=F32)
    mixed = jnp.dot(activated, contract_ref[...], preferred_element_type=F32)
    total = attended + mixed
    half = pl.num_programs(0) // 2

    @pl.when(step < half)
    def _():
        peer_ref[...] = bf16(total)

    @pl.when(step >= half)
    def _():
        own_ref[...] = total


def forward(meta, two, context, output, vecs, pieces, copies_of):
    rows = two.shape[0]
    half_ff = FF // 2
    count = len(pieces)
    steps = rows // ROWS
    half = steps // 2
    whole = lambda i, m: (0, 0)
    turned = lambda i, m: (lax.rem(i + half, steps), 0)
    weight_specs = [
        pl.BlockSpec((D, half_ff), whole),
        pl.BlockSpec((half_ff, D), whole),
    ]
    out_specs = [
        pl.BlockSpec((ROWS, half_ff), turned),
        pl.BlockSpec((ROWS, half_ff), turned),
        pl.BlockSpec((ROWS, D), lambda i, m: (jnp.minimum(i, half - 1), 0)),
        pl.BlockSpec((ROWS, D), lambda i, m: (jnp.maximum(i - half, 0), 0)),
    ]
    out_shape = [
        jax.ShapeDtypeStruct((rows, half_ff), BF16),
        jax.ShapeDtypeStruct((rows, half_ff), F32),
        jax.ShapeDtypeStruct((rows // 2, D), BF16),
        jax.ShapeDtypeStruct((rows // 2, D), F32),
    ]
    piece_specs = weight_specs
    if copies_of is not None:
        out_specs = out_specs + weight_specs
        out_shape += [
            jax.ShapeDtypeStruct((D, half_ff), BF16),
            jax.ShapeDtypeStruct((half_ff, D), BF16),
        ]
        piece_specs = [pl.BlockSpec(memory_space=pltpu.VMEM)] * count
        pieces = in_memory(pltpu.VMEM, pieces)
    return pl.pallas_call(
        partial(forward_kernel, copies_of, count),
        grid_spec=pltpu.PrefetchScalarGridSpec(
            num_scalar_prefetch=1,
            grid=(steps,),
            in_specs=[
                pl.BlockSpec((ROWS, D), turned),
                pl.BlockSpec((ROWS, D // 2), turned),
                pl.BlockSpec((D // 2, D), whole),
                pl.BlockSpec((8, 3 * D), whole),
            ]
            + piece_specs,
            out_specs=out_specs,
        ),
        out_shape=out_shape,
        compiler_params=PARAMS,
        name="forward",
    )(meta, two, context, output, vecs, *pieces)


def backward_kernel(
    own, unit_ref, scale_ref, up_ref, slope_ref, scaled_ref, expand_ref, contract_ref, vec_ref,
    grad_ref, pulled_ref, sums_ref
):
    slope_grad = dot_last(up_ref[...], contract_ref[...])
    grad = bf16(slope_grad * slope_ref[...])
    grad_ref[...] = grad
    total = dot_last(grad, expand_ref[...])
    unit, scale = unit_ref[...], scale_ref[:, :1]
    scaled = scaled_ref[...] + total * vec_ref[2:3, :D]
    pulled = (
        scaled
        - jnp.mean(scaled, axis=-1, keepdims=True)
        - unit * jnp.mean(scaled * unit, axis=-1, keepdims=True)
    ) * scale
    if own:
        pulled = pulled + f32(up_ref[...])
    pulled_ref[...] = pulled.astype(pulled_ref.dtype)

    @pl.when(pl.program_id(0) == 0)
    def _():
        sums_ref[...] = jnp.zeros_like(sums_ref)

    sums_ref[0:1, :D] += jnp.sum(total * unit, axis=0, keepdims=True)
    sums_ref[1:2, :D] += jnp.sum(total, axis=0, keepdims=True)
    sums_ref[2:3, :] += jnp.sum(f32(grad), axis=0, keepdims=True)


def backward(unit, scale, up, slope, scaled, expand, contract, vecs, own):
    rows = up.shape[0]
    half_ff = FF // 2
    base = 0 if own else rows // ROWS
    whole = lambda i: (0, 0)
    block = lambda i: (i, 0)
    return pl.pallas_call(
        partial(backward_kernel, own),
        grid=(rows // ROWS,),
        in_specs=[
            pl.BlockSpec((ROWS, D), block),
            pl.BlockSpec((ROWS, LANES), block),
            pl.BlockSpec((ROWS, D), block),
            pl.BlockSpec((ROWS, half_ff), lambda i: (base + i, 0)),
            pl.BlockSpec((ROWS, D), block),
            pl.BlockSpec((D, half_ff), whole),
            pl.BlockSpec((half_ff, D), whole),
            pl.BlockSpec((8, 3 * D), whole),
        ],
        out_specs=[
            pl.BlockSpec((ROWS, half_ff), block),
            pl.BlockSpec((ROWS, D), block),
            pl.BlockSpec((8, half_ff), whole),
        ],
        out_shape=[
            jax.ShapeDtypeStruct((rows, half_ff), BF16),
            jax.ShapeDtypeStruct((rows, D), F32 if own else BF16),
            jax.ShapeDtypeStruct((8, half_ff), F32),
        ],
        compiler_params=PARAMS,
        name="backward_own" if own else "backward_peer",
    )(unit, scale, up, slope, scaled, expand, contract, vecs)


def weight_grads_kernel(ring, sums, meta_ref, left_own, left_peer, right_own, right_peer, *refs):
    parts, refs = refs[:sums], refs[sums:]
    keep_ref, sent_ref, total_ref = refs[0], refs[1] if ring else None, refs[2 if ring else 1]
    step = pl.program_id(0)

    def products():
        total_ref[...] = dot_rows(left_own[...], right_own[...]) + dot_rows(
            left_peer[...], right_peer[...]
        )

    if sums:
        vec_ref = refs[3]
        last = pl.num_programs(0) - 1
        pl.when(step < last)(products)

        @pl.when(step == last)
        def _():
            collect(meta_ref[16], *parts, vec_ref)
            depth = keep_ref.shape[1]
            width = vec_ref.shape[1]
            total_ref[...] = jnp.zeros_like(total_ref)
            values = vec_ref[...]
            for device in range(D // depth):

                def rolled(size):
                    shift = device * size
                    return pltpu.roll(values, width - shift, 1) if shift else values

                row = device * depth
                total_ref[row : row + 8, :LANES] = rolled(depth)[:, :LANES]
                bias = rolled(3 * depth)
                total_ref[row + 8 : row + 9, :LANES] = bias[5:6, :LANES]
                total_ref[row + 9 : row + 10, :LANES] = bias[5:6, LANES : 2 * LANES]
                total_ref[row + 16 : row + 18, :LANES] = rolled(2 * depth)[6:8, :LANES]

    else:
        products()
    spread(meta_ref, total_ref, keep_ref, sent_ref)


def weight_grads(meta, left, right, rows_each, shards, ring, sums=()):
    (left_own, left_peer, left_shift), (right_own, right_peer) = left, right
    rows = right_own.shape[0]
    depth = left_own.shape[1]
    block = 384
    steps = right_own.shape[1] // block
    columns = right_own.shape[1] + (LANES if sums else 0)
    specs, shapes = grads_out(columns, block, rows_each, shards, ring)
    column = lambda i, m: (0, jnp.minimum(i, steps - 1))
    scratch = [pltpu.VMEM((depth, block), F32)]
    if sums:
        scratch.append(pltpu.VMEM((8, 3 * D), F32))
    return pl.pallas_call(
        partial(weight_grads_kernel, ring, len(sums)),
        grid_spec=pltpu.PrefetchScalarGridSpec(
            num_scalar_prefetch=1,
            grid=(pl.cdiv(columns, block),),
            in_specs=[
                pl.BlockSpec((rows, depth), lambda i, m: (0, 0)),
                pl.BlockSpec((rows, depth), lambda i, m: (left_shift, 0)),
                pl.BlockSpec((rows, block), column),
                pl.BlockSpec((rows, block), column),
            ]
            + [pl.BlockSpec(part.shape, lambda i, m: (0, 0)) for part in sums],
            out_specs=specs,
            scratch_shapes=scratch,
        ),
        out_shape=shapes,
        compiler_params=PARAMS,
    )(meta, left_own, left_peer, right_own, right_peer, *sums)


def attention_kernel(
    side_ref, q_ref, k_ref, v_ref, own_ref, peer_ref, output_ref, tables_ref, *refs
):
    context_ref, grads_ref, dk_acc, dv_acc = refs[-4:]
    rows = q_ref.shape[0]
    half = rows // 2
    block = min(256, half)
    start_one = pl.multiple_of(side_ref[16] * half, half)
    start_two = pl.multiple_of((1 - side_ref[16]) * half, half)

    def natural(ref):
        return jnp.concatenate([ref[pl.ds(start_one, half), :], ref[pl.ds(start_two, half), :]], 0)

    q = natural(q_ref) * jnp.asarray(0.125, BF16)
    k = natural(k_ref)
    v = natural(v_ref)
    up_own = bf16(dot_last(own_ref[...], output_ref[...]))
    up_peer = bf16(dot_last(peer_ref[...], output_ref[...]))
    second = side_ref[16] == 1
    up = jnp.concatenate(
        [jnp.where(second, up_peer, up_own), jnp.where(second, up_own, up_peer)], 0
    )
    lane = lax.broadcasted_iota(jnp.int32, (1, LANES), 1)
    dk_acc[...] = jnp.zeros_like(dk_acc)
    dv_acc[...] = jnp.zeros_like(dv_acc)
    below = lax.broadcasted_iota(jnp.int32, (block, block), 0) <= lax.broadcasted_iota(
        jnp.int32, (block, block), 1
    )

    def rotate_back(values, start):
        cosine = tables_ref[0, pl.ds(start, values.shape[0]), :]
        plus = tables_ref[1, pl.ds(start, values.shape[0]), :]
        minus = tables_ref[2, pl.ds(start, values.shape[0]), :]
        return (
            values * cosine
            - pltpu.roll(values, LANES - 8, 1) * plus
            - pltpu.roll(values, 8, 1) * minus
        )

    def local(row):
        return pl.multiple_of(
            (start_one if row < half else start_two) + (row if row < half else row - half), block
        )

    def products(number, head):
        low, high = number * block, (number + 1) * block
        mask = (lane // HD == head).astype(BF16)
        q_head = q[low:high] * mask
        up_head = up[low:high] * mask
        return q_head, up_head, dot_last(k[:high], q_head), dot_last(v[:high], up_head)

    def soften(number, scores, weights_grad):
        low, high = number * block, (number + 1) * block
        diagonal = jnp.where(below, scores[low:high], -1e30)
        scores = diagonal if low == 0 else jnp.concatenate([scores[:low], diagonal], 0)
        highest = jnp.max(scores, axis=0, keepdims=True)
        expo = jnp.exp(scores - highest)
        total = jnp.sum(expo, axis=0, keepdims=True)
        probs = expo * (1.0 / total)
        inner = jnp.sum(probs * weights_grad, axis=0, keepdims=True)
        return bf16(probs), bf16(probs * (weights_grad - inner))

    heads = LANES // HD
    work = [(number, head) for number in range(rows // block) for head in range(heads)]
    sums = {}

    def outputs(number, head, q_head, up_head, weights, scores_grad):
        low, high = number * block, (number + 1) * block
        mine = slice(head * HD, (head + 1) * HD)
        context = dot_rows(v[:high, mine], weights)
        dq = dot_rows(k[:high, mine], scores_grad)
        dv_acc[:high, :] += jnp.dot(weights, up_head, preferred_element_type=F32)
        dk_acc[:high, :] += jnp.dot(scores_grad, q_head, preferred_element_type=F32)
        sums[head] = (context, dq)
        if head == heads - 1:
            context = jnp.concatenate([sums[h][0] for h in range(heads)], 0)
            dq = jnp.concatenate([sums[h][1] for h in range(heads)], 0)
            place = local(low)
            context_ref[pl.ds(place, block), :] = bf16(context.T)
            dq_low = f32(bf16(dq.T * 0.125))
            grads_ref[0, pl.ds(place, block), :] = bf16(rotate_back(dq_low, place))

    ready = products(*work[0])
    waiting = None
    for index, item in enumerate(work):
        q_head, up_head, scores, weights_grad = ready
        if index + 1 < len(work):
            ready = products(*work[index + 1])
        softened = soften(item[0], scores, weights_grad)
        if waiting is not None:
            outputs(*waiting)
        waiting = item + (q_head, up_head) + softened
    outputs(*waiting)
    for number in range(rows // block):
        low = number * block
        place = local(low)
        dk_low = dk_acc[low : low + block, :].astype(BF16).astype(F32)
        grads_ref[1, pl.ds(place, block), :] = rotate_back(dk_low, place).astype(BF16)
        grads_ref[2, pl.ds(place, block), :] = dv_acc[low : low + block, :].astype(BF16)


def attention(side, packed, own, peer, output, tables, number, count, before):
    rows, columns = packed.shape[0], packed.shape[1] // 3
    pairs = columns // LANES
    ins = [side, packed, packed, packed, own, peer, output, tables]
    return pl.pallas_call(
        attention_kernel,
        grid_spec=pltpu.PrefetchScalarGridSpec(
            num_scalar_prefetch=1,
            grid=(count,),
            in_specs=[
                pl.BlockSpec((rows, LANES), lambda i, s: (0, number + i)),
                pl.BlockSpec((rows, LANES), lambda i, s: (0, pairs + number + i)),
                pl.BlockSpec((rows, LANES), lambda i, s: (0, 2 * pairs + number + i)),
                pl.BlockSpec((rows // 2, D), lambda i, s: (0, 0)),
                pl.BlockSpec((rows // 2, D), lambda i, s: (0, 0)),
                pl.BlockSpec((LANES, D), lambda i, s: (number + i, 0)),
                pl.BlockSpec((3, rows, LANES), lambda i, s: (0, 0, 0)),
            ]
            + [pl.BlockSpec(memory_space=pl.ANY)] * len(before),
            out_specs=[
                pl.BlockSpec((rows, LANES), lambda i, s: (0, number + i)),
                pl.BlockSpec((3, rows, LANES), lambda i, s: (0, 0, number + i)),
            ],
            scratch_shapes=[pltpu.VMEM((rows, LANES), F32), pltpu.VMEM((rows, LANES), F32)],
        ),
        out_shape=[
            jax.ShapeDtypeStruct((rows, columns), BF16),
            jax.ShapeDtypeStruct((3, rows, columns), BF16),
        ],
        input_output_aliases={len(ins) + i: i for i in range(len(before))},
        compiler_params=PARAMS,
    )(*ins, *before)


def finish_first_kernel(side_ref, mine_ref, peer_ref, joint_ref, output_ref, contract_ref):
    side = side_ref[0]
    half_d = D // 2
    depth = mine_ref.shape[0]
    for source, plane in ((mine_ref, side), (peer_ref, 1 - side)):
        for part in range(3):
            start = pl.multiple_of(part * D + plane * half_d, LANES)
            joint_ref[:, pl.ds(start, half_d)] = f32(
                source[:, part * half_d : (part + 1) * half_d]
            )
        for part in range(2):
            start = pl.multiple_of((plane * 2 + part) * depth, depth)
            columns = slice(5 * half_d + part * D, 5 * half_d + (part + 1) * D)
            contract_ref[pl.ds(start, depth), :] = f32(source[:, columns])
    columns = slice(3 * half_d, 5 * half_d)
    output_ref[...] = mine_ref[:, columns] + f32(peer_ref[:, columns])


def finish_first(side, mine, peer):
    depth = mine.shape[0]
    whole = lambda i, s: (0, 0)
    shapes = [(depth, 3 * D), (depth, D), (4 * depth, D)]
    return pl.pallas_call(
        finish_first_kernel,
        grid_spec=pltpu.PrefetchScalarGridSpec(
            num_scalar_prefetch=1,
            grid=(1,),
            in_specs=[pl.BlockSpec(mine.shape, whole), pl.BlockSpec(peer.shape, whole)],
            out_specs=[pl.BlockSpec(shape, whole) for shape in shapes],
        ),
        out_shape=[jax.ShapeDtypeStruct(shape, F32) for shape in shapes],
        compiler_params=PARAMS,
        name="finish_first",
    )(side, mine, peer)


def finish_expand_kernel(shards, side_ref, mine_ref, peer_ref, expand_ref, *outs):
    half_ff = FF // 2
    wide = half_ff // shards
    depth = mine_ref.shape[0]
    here = side_ref[0] == 0
    mine, peer = mine_ref[:, :half_ff], f32(peer_ref[:, :half_ff])
    zero, one = jnp.where(here, mine, peer), jnp.where(here, peer, mine)
    for device in range(shards):
        columns = slice(device * wide, (device + 1) * wide)
        expand_ref[:, 2 * device * wide : (2 * device + 1) * wide] = zero[:, columns]
        expand_ref[:, (2 * device + 1) * wide : (2 * device + 2) * wide] = one[:, columns]
    tile = mine_ref[:, half_ff:] + f32(peer_ref[:, half_ff:])
    outs[7][...] = tile[4:5, :depth]
    for row in range(5):
        outs[row][...] = tile[row : row + 1, :depth]
    outs[5][:, :LANES] = tile[8:9, :]
    outs[5][:, LANES:] = tile[9:10, : 3 * depth - LANES]
    outs[6][:, :wide] = tile[16:17, :wide]
    outs[6][:, wide:] = tile[17:18, :wide]


def finish_expand(side, mine, peer, shards):
    depth = mine.shape[0]
    whole = lambda i, s: (0, 0)
    shapes = [(depth, FF)] + [(1, depth)] * 5 + [(1, 3 * depth), (1, FF // shards), (1, depth)]
    outs = pl.pallas_call(
        partial(finish_expand_kernel, shards),
        grid_spec=pltpu.PrefetchScalarGridSpec(
            num_scalar_prefetch=1,
            grid=(1,),
            in_specs=[pl.BlockSpec(mine.shape, whole), pl.BlockSpec(peer.shape, whole)],
            out_specs=[pl.BlockSpec(shape, whole) for shape in shapes],
        ),
        out_shape=[jax.ShapeDtypeStruct(shape, F32) for shape in shapes],
        compiler_params=PARAMS,
        name="finish_expand",
    )(side, mine, peer)
    return outs[0], [out.reshape(-1) for out in outs[1:]]


def finish_out_kernel(tokens_ref, mine_ref, peer_ref, vec_ref, out_ref):
    out_ref[...] = bf16(
        f32(tokens_ref[...]) + mine_ref[...] + f32(peer_ref[...]) + vec_ref[4:5, :D]
    )


def finish_tokens_kernel(mine_ref, peer_ref, out_ref):
    out_ref[...] = mine_ref[...] + f32(peer_ref[...])


def finish_rows(kernel, ins, kept):
    rows = ins[0].shape[0]
    block = lambda i: (i, 0)
    specs = [pl.BlockSpec((ROWS // 2, D), block) for _ in ins[:3]]
    if len(ins) > 3:
        specs.append(pl.BlockSpec(ins[3].shape, lambda i: (0, 0)))
    return pl.pallas_call(
        kernel,
        grid=(rows // (ROWS // 2),),
        in_specs=specs,
        out_specs=pl.BlockSpec((ROWS // 2, D), block),
        out_shape=jax.ShapeDtypeStruct((rows, D), kept),
        compiler_params=PARAMS,
    )(*ins)


def layer(
    tokens,
    first_norm_gain,
    first_norm_shift,
    second_norm_gain,
    second_norm_shift,
    projection_weight,
    projection_bias,
    output_weight,
    output_bias,
    expand_weight,
    expand_bias,
    contract_weight,
    contract_bias,
    cotangent,
):
    shards = lax.axis_size("fsdp")
    ring = shards == RING_SIZE
    me = lax.axis_index("fsdp").astype(jnp.int32)
    side = lax.axis_index("seq").astype(jnp.int32)
    rows = tokens.shape[1]
    depth = D // shards
    wide = FF // shards // 2
    half_d, half_ff = D // 2, FF // 2
    split = 3 * half_d
    here = side == 0

    own_tokens, own_up = tokens[0], cotangent[0]
    peer_tokens = side_swap(own_tokens)
    peer_up = side_swap(own_up)

    vectors = [
        first_norm_gain,
        first_norm_shift,
        second_norm_gain,
        second_norm_shift,
        output_bias,
        contract_bias,
    ]

    def feed_forward_halves(expand_weight, contract_weight):
        by_side = expand_weight.reshape(depth, shards, 2, wide)
        expand_half = jnp.where(here, by_side[:, :, 0], by_side[:, :, 1])
        contract_half = jnp.where(here, contract_weight[:wide], contract_weight[wide:])
        return expand_half.reshape(depth, half_ff), contract_half

    first_copies = second_copies = None
    row_start = side * rows
    if ring:
        order = lax.dynamic_index_in_dim(jnp.asarray(ring_table()), me, 0, keepdims=False)
        meta = jnp.concatenate([order, side.reshape(1)])
        first_shard = pack(
            side.reshape(1), projection_weight, output_weight, vectors, projection_bias, expand_bias
        )
        middle = 8 * LANES
        first_pieces = ring_gather(first_shard, 1, middle)
        expand_weight, row_start, first_pieces[1] = lax.optimization_barrier(
            (expand_weight, row_start, first_pieces[1])
        )
        expand_half, contract_half = feed_forward_halves(expand_weight, contract_weight)
        second_shard = jnp.concatenate(
            [expand_half[:, :D], expand_half[:, D:], contract_half], 0
        )
        second_pieces = ring_gather(second_shard, 0, 2 * depth)

        def first_copies(part, device):
            lines = device_rows(device, depth)
            every = pl.ds(0, depth)
            if part == "a":
                return [((every, pl.ds(0, middle)), 0, (lines, pl.ds(0, middle)))]
            shift = middle if part == "b" else 0
            return [
                ((every, pl.ds(0, split - shift)), 0, (lines, pl.ds(shift, split - shift))),
                ((every, pl.ds(split - shift, D)), 1, (lines, pl.ds(0, D))),
                ((every, pl.ds(split - shift + D, LANES)), 2, (lines, pl.ds(0, LANES))),
            ]

        def second_copies(part, device):
            lines = device_rows(device, depth)
            low = ((pl.ds(0, depth), pl.ds(0, D)), 0, (lines, pl.ds(0, D)))
            high = ((pl.ds(depth, depth), pl.ds(0, D)), 0, (lines, pl.ds(D, D)))
            start = 0 if part == "b" else 2 * depth
            last = ((pl.ds(start, wide), pl.ds(0, D)), 1, (device_rows(device, wide), pl.ds(0, D)))
            return {"all": [low, high, last], "a": [low, high], "b": [last]}[part]

    else:
        gather = partial(lax.all_gather, axis_name="fsdp", axis=0, tiled=True)
        expand_half, contract_half = feed_forward_halves(expand_weight, contract_weight)
        meta = jnp.concatenate([jnp.zeros((16,), jnp.int32), side.reshape(1)])
        by_half = projection_weight.reshape(depth, 3, 2, half_d)
        projection_half = jnp.where(here, by_half[:, :, 0], by_half[:, :, 1])
        first_full = gather(
            jnp.concatenate([projection_half.reshape(depth, split), output_weight], 1)
        )
        gathered = [f32(gather(v)) for v in vectors]
        shift = gather(expand_bias).reshape(shards, 2, wide)
        vecs = jnp.zeros((8, 3 * D), F32)
        for row, value in enumerate(gathered[:4]):
            vecs = vecs.at[row, :D].set(value)
        vecs = vecs.at[4, :D].set(gathered[4] + gathered[5])
        vecs = vecs.at[5].set(f32(gather(projection_bias)))
        for part in range(2):
            vecs = vecs.at[6 + part, :half_ff].set(f32(shift[:, part].reshape(half_ff)))
        first_pieces = [first_full, vecs]
        second_pieces = [gather(expand_half), gather(contract_half)]

    row_numbers = jnp.arange(rows, dtype=jnp.int32)
    positions = jnp.concatenate([row_start + row_numbers, rows - row_start + row_numbers])
    tables = rotary_lanes(positions)
    unit_own, scale_own = units(own_tokens)
    unit_peer, scale_peer = units(peer_tokens)
    packed, one, two, projection_full, output_half, vecs = project(
        meta, unit_own, unit_peer, tables, first_pieces, first_copies
    )
    attend = partial(attention, meta, packed, own_up, peer_up, output_half, tables)
    context, grads = attend(1, half_d // LANES - 1, attend(0, 1, ()))
    joint_parts = list(
        joint_grads(meta, one, grads, context, own_up, peer_up, depth, shards, ring)
    )
    context, joint_parts[-1] = lax.optimization_barrier((context, joint_parts[-1]))
    forward_parts = forward(meta, two, context, output_half, vecs, second_pieces, second_copies)
    act, slope, out_peer, out_own = forward_parts[:4]
    expand_full, contract_full = forward_parts[4:] if ring else second_pieces
    out_arrived = side_swap(out_peer)
    contract_parts = list(
        contract_grads(meta, act, own_up, peer_up, depth, shards, ring)
    )
    grads, contract_parts[-1] = lax.optimization_barrier((grads, contract_parts[-1]))
    if ring:
        first, first_low = ring_scatter([joint_parts, contract_parts], 14 * LANES)
        first_peer = side_swap(first_low)
    else:
        scatter = partial(lax.psum_scatter, axis_name="fsdp", scatter_dimension=0, tiled=False)
        first = jnp.concatenate([scatter(joint_parts[0]), scatter(contract_parts[0])], 1)
        first_peer = side_swap(bf16(first))

    scaled_peer, one_peer = joint_back(unit_peer, peer_up, grads, projection_full, vecs, False)
    grads, scaled_peer = lax.optimization_barrier((grads, scaled_peer))
    scaled_own, one_own = joint_back(unit_own, own_up, grads, projection_full, vecs, True)
    scaled_peer, scaled_own = lax.optimization_barrier((scaled_peer, scaled_own))
    weights = (expand_full, contract_full, vecs)
    grad_peer, pulled_peer, sums_peer = backward(
        unit_peer, scale_peer, peer_up, slope, scaled_peer, *weights, False
    )
    scaled_own, pulled_peer = lax.optimization_barrier((scaled_own, pulled_peer))
    pulled_arrived = side_swap(pulled_peer)
    grad_own, pulled_own, sums_own = backward(
        unit_own, scale_own, own_up, slope, scaled_own, *weights, True
    )
    sums = (one_peer, one_own, sums_peer, sums_own)
    expand_parts = weight_grads(
        meta, (two, two, 1), (grad_own, grad_peer), depth, shards, ring, sums if ring else ()
    )
    if ring:
        expand, expand_low = ring_scatter([expand_parts], 7 * LANES)
        expand_peer = side_swap(expand_low)
    else:
        expand = scatter(expand_parts[0])
        expand_peer = side_swap(bf16(expand))

    layer_output = finish_rows(
        finish_out_kernel, [own_tokens, out_own, out_arrived, vecs], BF16
    )[None]
    tokens_grad = finish_rows(finish_tokens_kernel, [pulled_own, pulled_arrived], F32)[None]
    if ring:
        joint_grad, output_grad, contract_grad = finish_first(side.reshape(1), first, first_peer)
        expand_grad, picked = finish_expand(side.reshape(1), expand, expand_peer, shards)
    else:
        peer = f32(first_peer)
        zero, other = jnp.where(here, first, peer), jnp.where(here, peer, first)
        joint_grad = jnp.stack(
            [
                zero[:, :split].reshape(depth, 3, half_d),
                other[:, :split].reshape(depth, 3, half_d),
            ],
            2,
        ).reshape(depth, 3 * D)
        output_grad = (first + peer)[:, split : split + D]
        last = split + D
        contract_grad = jnp.concatenate(
            [zero[:, last : last + D], zero[:, last + D :], other[:, last : last + D], other[:, last + D :]],
            0,
        )
        peer = f32(expand_peer)
        zero, other = jnp.where(here, expand, peer), jnp.where(here, peer, expand)
        expand_grad = jnp.stack(
            [zero.reshape(depth, shards, wide), other.reshape(depth, shards, wide)], 2
        ).reshape(depth, FF)
        small = lax.psum(collect_sums(meta, *sums), ("fsdp", "seq"))

        def own_part(row, size):
            return lax.dynamic_slice(small, (row, me * size), (1, size))[0]

        picked = [own_part(row, depth) for row in range(5)]
        picked.append(own_part(5, 3 * depth))
        picked.append(jnp.concatenate([own_part(6, wide), own_part(7, wide)]))
        picked.append(picked[4])
    gain_one, shift_one, gain_two, shift_two, bias, joint_bias, expand_bias_grad, bias_again = picked
    return (
        layer_output,
        tokens_grad,
        gain_one,
        shift_one,
        gain_two,
        shift_two,
        joint_grad,
        joint_bias,
        output_grad,
        bias,
        expand_grad,
        expand_bias_grad,
        contract_grad,
        bias_again,
    )


def solution(mesh):
    return jax.shard_map(
        layer,
        mesh=mesh,
        in_specs=(
            P("fsdp", "seq", None),
            P("fsdp"),
            P("fsdp"),
            P("fsdp"),
            P("fsdp"),
            P("fsdp", None),
            P("fsdp"),
            P("fsdp", None),
            P("fsdp"),
            P("fsdp", None),
            P("fsdp"),
            P("fsdp", None),
            P("fsdp"),
            P("fsdp", "seq", None),
        ),
        out_specs=(
            P("fsdp", "seq", None),
            P("fsdp", "seq", None),
            P("fsdp"),
            P("fsdp"),
            P("fsdp"),
            P("fsdp"),
            P("fsdp", None),
            P("fsdp"),
            P("fsdp", None),
            P("fsdp"),
            P("fsdp", None),
            P("fsdp"),
            P("fsdp", None),
            P("fsdp"),
        ),
        check_vma=False,
    )
```
